512 devices in a mesh: tiles: 128 (over x, y_lo, z, core), bins: 4 (over y_hi).
Axes of the slice: x: 4, y: 8 (y_hi: 4, y_lo: 2; y = y_hi * 2 + y_lo), z: 8, core: 2. Of those that a mesh axis runs over, the one named last changes fastest.
Arguments:
- dust_state: float32 [4, 112, 512, 256], P(None, 'bins', 'tiles'), may hold values from -4 to 4, as said below
- drift_speed: float32 [112], P('bins'), may hold values from -0.5 to 0.5
- stop_ratio: float32 [112], P('bins'), may hold values from 0.05 to 20
- gas_rho: float32 [512, 256], P('tiles'), may hold values from 0.5 to 2
- gas_vel: float32 [3, 512, 256], P(None, 'tiles'), may hold values from -3 to 3
- pressure: float32 [512, 256], P('tiles'), may hold values from 0.5 to 2
- pair_list: int32 [6328, 2], replicated, may hold values from 0 to 111, as said below
- outcome: float32 [6328, 112], P(None, 'bins'), may hold values from -0.078125 to 0.078125
Outputs:
- dust_next: float32 [4, 112, 512, 256], P(None, 'bins', 'tiles')
The draws below stay inside these ranges and needn't reach their ends.
Inputs may be any that keep to these rules, and one draw needn't show every extreme that they name: `dust_state`: field 0 lies in 0.3 to 3. `pair_list`: each unordered pair of bins, a bin with itself included, stands once, smaller bin first.
All inputs are finite; a program needn't handle non-finite values.
Results may differ from the reference program's by a relative error of at most 0.000065.
Values sent between devices are 32-bit elements; how exact they have to be, the bound alone decides.
A program may use at most 64 MiB of HBM per device.

```python
import math
import jax
import jax.numpy as jnp
import numpy as np
from jax import lax

NB = 112
NPAIR = 6328
CY = 256
NX = 512


def draw_dust_state(key, part):
    density_key, momenta_key = jax.random.split(jax.random.fold_in(key, 11))
    density = jnp.exp(jax.random.uniform(density_key, (1, NB, NX, CY), jnp.float32, math.log(0.3), math.log(3.0)))
    momenta = jnp.clip(jax.random.normal(momenta_key, (3, NB, NX, CY), jnp.float32), -4.0, 4.0)
    return jnp.concatenate([density, momenta], 0)


def draw_pair_list(key, part):
    upper_pairs = np.triu_indices(NB)
    canonical = jnp.stack([jnp.asarray(upper_pairs[0]), jnp.asarray(upper_pairs[1])], axis=1).astype(jnp.int32)
    shuffled = jax.random.permutation(jax.random.fold_in(key, 5), NPAIR)
    return canonical[shuffled]


def levels(stream_key, extent, pieces, low, top_value):
    gain, own = 1.0, jax.random.fold_in(stream_key, 6)
    for dim, blocks in pieces:
        steps = jnp.exp(jax.random.uniform(jax.random.fold_in(own, dim), (blocks,), jnp.float32, low / len(pieces), top_value / len(pieces)))
        gain = gain * jnp.repeat(steps, extent[dim] // blocks).reshape([-1 if axis == dim else 1 for axis in range(len(extent))])
    return gain


def scatter_about(own_key, shape, width, limit, shards=(), kind=jnp.bfloat16):
    result = jax.random.normal(own_key, shape, jnp.float32) * width
    if len(shards) > 0:
        result = levels(own_key, shape, shards, -0.22, 0.18) * result
    return jnp.clip(result, min=-limit, max=limit).astype(kind)


def setup_inputs(seed: int = 0) -> dict:
    key_list = jax.random.split(jax.random.key(seed), 9)
    return {
        "dust_state": draw_dust_state(jax.random.fold_in(key_list[8], 71), 0),
        "drift_speed": jnp.clip(jax.random.uniform(key_list[1], (NB,), jnp.float32, -0.5, 0.5) * levels(key_list[1], (NB,), ((0, 4),), -0.4, 0.0), -0.5, 0.5),
        "stop_ratio": jnp.clip(jnp.exp(math.log(20.0) - 5.9914645 * jax.random.uniform(key_list[2], (NB,), jnp.float32) ** levels(key_list[2], (NB,), ((0, 4),), -0.2, 0.2)), 0.05, 20.0),
        "gas_rho": jnp.clip(jnp.exp(math.log(2.0) - 1.3862944 * jax.random.uniform(key_list[3], (NX, CY), jnp.float32) ** levels(key_list[3], (NX, CY), ((0, 128),), -0.2, 0.2)), 0.5, 2.0),
        "gas_vel": scatter_about(key_list[4], (3, NX, CY), 0.5, 3.0, ((1, 128),), jnp.float32),
        "pressure": jnp.clip(0.5 + 1.5 * jax.random.uniform(key_list[5], (NX, CY), jnp.float32) ** levels(key_list[5], (NX, CY), ((0, 128),), -0.2, 0.2), 0.5, 2.0),
        "pair_list": draw_pair_list(jax.random.fold_in(key_list[8], 71), 0),
        "outcome": scatter_about(key_list[7], (NPAIR, NB), NPAIR ** -0.5, 0.078125, ((1, 4),), jnp.float32),
    }


coag_step = 0.5
pressure_coupling = 1.0


def flux_rate(padded, courant):
    upwind_pos = jnp.maximum(courant, 0.0)[None, :, None, None]
    upwind_neg = jnp.minimum(courant, 0.0)[None, :, None, None]
    minus_two = padded[:, :, :-4]
    minus_one = padded[:, :, 1:-3]
    centre = padded[:, :, 2:-2]
    plus_one = padded[:, :, 3:-1]
    plus_two = padded[:, :, 4:]
    face_upper = upwind_pos * (1.5 * centre - 0.5 * minus_one) + upwind_neg * (1.5 * plus_one - 0.5 * plus_two)
    face_lower = upwind_pos * (1.5 * minus_one - 0.5 * minus_two) + upwind_neg * (1.5 * centre - 0.5 * plus_one)
    return face_lower - face_upper


def advect(state, courant):
    padded = jnp.pad(state, ((0, 0), (0, 0), (2, 2), (0, 0)))
    return flux_rate(padded, courant)


def coagulate(density, pair_list, outcome):
    flattened = density.reshape(NB, -1)
    cell_count = flattened.shape[1]
    block_size = 1024 if cell_count % 1024 == 0 else cell_count
    blocks = flattened.reshape(NB, cell_count // block_size, block_size).transpose(1, 0, 2)

    def one_block(part_block):
        first_bins = part_block[pair_list[:, 0]]
        second_bins = part_block[pair_list[:, 1]]
        return jnp.dot(outcome.T, first_bins * second_bins, precision=lax.Precision.HIGHEST, preferred_element_type=jnp.float32)

    gained = lax.map(one_block, blocks)
    return gained.transpose(1, 0, 2).reshape(density.shape)


def reference(dust_state, drift_speed, stop_ratio, gas_rho, gas_vel, pressure, pair_list, outcome):
    section_one = dust_state + advect(dust_state, drift_speed)
    moved = 0.5 * (dust_state + section_one + advect(section_one, drift_speed))
    source = coagulate(moved[0], pair_list, outcome)
    density = moved[0] + coag_step * source
    grown = moved[1:] + coag_step * source[None] * gas_vel[:, None]
    padded_pressure = jnp.pad(pressure, ((1, 1), (0, 0)))
    gradient = (padded_pressure[2:] - padded_pressure[:-2]) / (2.0 * gas_rho)
    target = jnp.concatenate([(gas_vel[0] - pressure_coupling * gradient)[None], gas_vel[1:]], 0)
    coupling = stop_ratio[None, :, None, None]
    momenta = (grown + coupling * density[None] * target[:, None]) / (1.0 + coupling)
    return jnp.concatenate([density[None], momenta], 0)
```

```python
import functools

import jax
import jax.numpy as jnp
from jax import lax
from jax.experimental import pallas as pl
from jax.experimental.pallas import tpu as pltpu
from jax.sharding import PartitionSpec as P

MESH = pl.DeviceIdType.MESH
BINS = 112
LOCAL = 28
PAIRS = 6328
PADDED = 6400
ZERO_ROW = PADDED - 1
GROUPS = 7
f32, bf16, i32 = jnp.float32, jnp.bfloat16, jnp.int32


def bin_at(group, member):
    if group < 6:
        tile = 2 * group + member // 8
        return tile // 3, (tile % 3) * 8 + member % 8
    return member // 4, 24 + member % 4


def group_member(index):
    shard = (index >= 28).astype(i32) + (index >= 56).astype(i32) + (index >= 84).astype(i32)
    own = index - 28 * shard
    tile = 3 * shard + (own >> 3)
    full = own < 24
    group = jnp.where(full, tile >> 1, 6)
    member = jnp.where(full, ((tile & 1) << 3) + (own & 7), 4 * shard + own - 24)
    return group, member


def slots_of(pairs):
    group_i, member_i = group_member(pairs[0:1, :])
    group_j, member_j = group_member(pairs[1:2, :])
    ahead = group_j - group_i
    ahead = jnp.where(ahead < 0, ahead + GROUPS, ahead)
    keep = ahead <= 3
    row = jnp.where(keep, group_i * 16 + member_i, group_j * 16 + member_j)
    slot = jnp.where(keep, ahead * 16 + member_j, (GROUPS - ahead) * 16 + member_i)
    return row, slot


def invert_pairs(pairs_ref, table_ref):
    total = jnp.zeros((BINS, 128), f32)
    for start in range(0, PAIRS, 256):
        width = min(256, PAIRS - start)
        row, slot = slots_of(pairs_ref[:, start : start + width])
        rows = lax.broadcasted_iota(i32, (BINS, width), 0)
        lanes = lax.broadcasted_iota(i32, (128, width), 0)
        number = start + 1 + lax.broadcasted_iota(i32, (1, width), 1)
        high = (number >> 6).astype(f32)
        low = (number & 63).astype(f32)
        value = jnp.where(lanes < 64, high, low)
        first = jnp.where(rows == row, 1.0, 0.0).astype(bf16)
        second = jnp.where((lanes & 63) == slot, value, 0.0).astype(bf16)
        total += lax.dot_general(first, second, (((1,), (1,)), ((), ())), preferred_element_type=f32)
    number = total * 64.0 + pltpu.roll(total, 64, 1)
    number = number.astype(i32)
    table_ref[...] = jnp.where(number > 0, number - 1, ZERO_ROW)


def turn_outcome(outcome_ref, turned_ref):
    for start in range(0, PAIRS, 128):
        width = min(128, PAIRS - start)
        turned_ref[start : start + width, 0:LOCAL] = outcome_ref[:, start : start + width].T
    turned_ref[PAIRS:PADDED, :] = jnp.zeros((PADDED - PAIRS, 128), f32)


def gather_two(table, turned_ref, held_ref, two):
    for half in range(2):
        for slot in range(64):
            at = half * 64 + slot
            index = table[2 * two + half, slot]
            held_ref[at : at + 1, :] = turned_ref[pl.ds(index, 1), :]


def place_two(held_ref, rates_ref, two):
    value = held_ref[...].T[0:32, :]
    high = value.astype(bf16).astype(f32)
    low = pltpu.roll(value - high, 64, 1)
    left = lax.broadcasted_iota(i32, (32, 128), 1) < 64
    start = pl.multiple_of(two * 64, 64)
    rates_ref[pl.ds(start, 32), :] = jnp.where(left, high, low).astype(bf16)
    rates_ref[pl.ds(start + 32, 32), :] = jnp.where(left, low, high).astype(bf16)


def sort_kernel(outcome_ref, pairs_ref, rates_ref, turned, held_a, held_b, table_v, table, sem):
    invert_pairs(pairs_ref, table_v)
    copy = pltpu.make_async_copy(table_v, table, sem)
    copy.start()
    turn_outcome(outcome_ref, turned)
    copy.wait()
    gather_two(table, turned, held_a, 0)

    def step(i, carry):
        gather_two(table, turned, held_b, 2 * i + 1)
        place_two(held_a, rates_ref, 2 * i)
        gather_two(table, turned, held_a, jnp.minimum(2 * i + 2, 55))
        place_two(held_b, rates_ref, 2 * i + 1)
        return carry

    lax.fori_loop(0, 28, step, 0)


def transported(own, before, after, speed):
    forward = jnp.maximum(speed, 0.0)
    backward = jnp.maximum(-speed, 0.0)

    def weights(a):
        square = a * a
        return (2.0 * a - 3.0 * square, 2.75 * square - 0.5 * a, -square, 0.125 * square)

    a = forward + backward
    row = lax.broadcasted_iota(i32, (8, 128), 0) & 3
    result = (1.0 - 1.5 * a + 1.125 * (a * a)) * own
    up, down = weights(forward), weights(backward)
    for m in (1, 2, 3):
        result += up[m - 1] * jnp.where(row >= m, pltpu.roll(own, m, 0), pltpu.roll(before, 4 + m, 0))
        result += down[m - 1] * jnp.where(row < 4 - m, pltpu.roll(own, 8 - m, 0), pltpu.roll(after, 4 - m, 0))
    return result + up[3] * before + down[3] * after


def step_kernel(
    dust, speed, stop, rho, vel, pres, rates, out,
    own, before, after, pres_before, pres_after, dens, high, low, source,
    own_sem, up_send, up_recv, down_send, down_recv, ring_send, ring_recv,
):
    tile, shard = lax.axis_index("tiles"), lax.axis_index("bins")
    tiles, shards = lax.axis_size("tiles"), lax.axis_size("bins")
    has_before, has_after = tile > 0, tile < tiles - 1
    nxt, prv = lax.rem(shard + 1, shards), lax.rem(shard + shards - 1, shards)

    own_copies = [
        pltpu.make_async_copy(dust.at[0:1], own.at[0:1], own_sem.at[0]),
        pltpu.make_async_copy(dust.at[1:4], own.at[1:4], own_sem.at[1]),
    ]
    for copy in own_copies:
        copy.start()

    barrier = pltpu.get_barrier_semaphore()
    pl.semaphore_signal(barrier, inc=1, device_id={"bins": nxt}, device_id_type=MESH)
    pl.semaphore_signal(barrier, inc=1, device_id={"bins": prv}, device_id_type=MESH)

    @pl.when(has_before)
    def _():
        pl.semaphore_signal(barrier, inc=1, device_id={"tiles": tile - 1}, device_id_type=MESH)

    @pl.when(has_after)
    def _():
        pl.semaphore_signal(barrier, inc=1, device_id={"tiles": tile + 1}, device_id_type=MESH)

    pl.semaphore_wait(barrier, 2 + has_before.astype(i32) + has_after.astype(i32))

    def tile_copies(send, recv, target, there, pres_there):
        make = functools.partial(pltpu.make_async_remote_copy, device_id={"tiles": target}, device_id_type=MESH)
        return [
            make(dust.at[0:1], there.at[0:1], send.at[0], recv.at[0]),
            make(pres, pres_there, send.at[1], recv.at[1]),
            make(dust.at[1:4], there.at[1:4], send.at[2], recv.at[2]),
        ]

    ups = tile_copies(up_send, up_recv, tile + 1, before, pres_before)
    downs = tile_copies(down_send, down_recv, tile - 1, after, pres_after)

    for part in range(3):
        @pl.when(has_after)
        def _():
            ups[part].start()

        @pl.when(has_before)
        def _():
            downs[part].start()

    @pl.when(jnp.logical_not(has_before))
    def _():
        before[...] = jnp.zeros_like(before)
        pres_before[...] = jnp.zeros_like(pres_before)

    @pl.when(jnp.logical_not(has_after))
    def _():
        after[...] = jnp.zeros_like(after)
        pres_after[...] = jnp.zeros_like(pres_after)

    def arrived(part):
        @pl.when(has_before)
        def _():
            ups[part].wait_recv()

        @pl.when(has_after)
        def _():
            downs[part].wait_recv()

    own_copies[0].wait()
    arrived(0)
    here = shard * 224
    for k in range(LOCAL):
        moved = transported(own[0, k], before[0, k], after[0, k], jnp.full((8, 128), speed[k], f32))
        out[0, k] = moved
        dens[pl.ds(here + k, 8, stride=LOCAL), :] = moved

    def ring_copy(block, half, target, slot):
        piece = dens.at[pl.ds(pl.multiple_of(block * 224 + half * 112, 16), 112), :]
        return pltpu.make_async_remote_copy(
            piece, piece, ring_send.at[slot], ring_recv.at[slot],
            device_id={"bins": target}, device_id_type=MESH,
        )

    two_back = lax.rem(shard + 2, shards)
    sends = [
        ring_copy(shard, 0, nxt, 0),
        ring_copy(shard, 1, prv, 1),
        ring_copy(shard, 1, nxt, 2),
        ring_copy(shard, 0, prv, 3),
    ]
    from_prv0 = ring_copy(prv, 0, nxt, 0)
    from_nxt1 = ring_copy(nxt, 1, prv, 1)
    from_prv1 = ring_copy(prv, 1, nxt, 2)
    from_nxt0 = ring_copy(nxt, 0, prv, 3)
    relay0 = ring_copy(prv, 0, nxt, 4)
    relay1 = ring_copy(nxt, 1, prv, 5)
    far0 = ring_copy(two_back, 0, nxt, 4)
    far1 = ring_copy(two_back, 1, prv, 5)
    for copy in sends:
        copy.start()

    own_copies[1].wait()
    arrived(1)
    arrived(2)

    def momenta(k, carry):
        rate = jnp.full((8, 128), speed[k], f32)
        for d in range(1, 4):
            out[d, k] = transported(own[d, k], before[d, k], after[d, k], rate)
        return carry

    lax.fori_loop(0, LOCAL, momenta, 0)

    from_prv0.wait_recv()
    relay0.start()
    from_nxt1.wait_recv()
    relay1.start()
    from_prv1.wait_recv()
    from_nxt0.wait_recv()
    far0.wait_recv()
    far1.wait_recv()

    for m in range(8):
        for group in range(GROUPS):
            if group < 6:
                starts = [bin_at(group, 0), bin_at(group, 8)]
                pieces = [dens[b * 224 + m * 28 + w : b * 224 + m * 28 + w + 8, :] for b, w in starts]
            else:
                pieces = [dens[b * 224 + m * 28 + 24 : b * 224 + m * 28 + 28, :] for b in range(4)]
            value = jnp.concatenate(pieces, 0)
            top = value.astype(bf16)
            rest = (value - top.astype(f32)).astype(bf16)
            for at in (group, group + GROUPS):
                if at < 10:
                    high[at * 16 : at * 16 + 16, m * 128 : m * 128 + 128] = top
                    low[at * 16 : at * 16 + 16, m * 128 : m * 128 + 128] = rest

    def columns(c, carry):
        cols = pl.ds(pl.multiple_of(c * 256, 256), 256)
        total = jnp.zeros((32, 256), f32)
        for group in range(GROUPS):
            window = pl.ds(group * 16, 64)
            top, rest = high[window, cols], low[window, cols]
            weights = jnp.concatenate([top, top, rest, rest], 0)
            block = rates[group * 512 : group * 512 + 512, :]
            product = jnp.dot(jnp.concatenate([block, block], 1), weights, preferred_element_type=f32)
            for member in range(16):
                b, w = bin_at(group, member)
                first = dens[pl.ds(b * 224 + w + c * 56, 1), :]
                second = dens[pl.ds(b * 224 + w + 28 + c * 56, 1), :]
                line = jnp.concatenate([first, second], 1)
                total += product[member * 32 : member * 32 + 32, :] * line
        for half in range(2):
            for k in range(4):
                source[pl.ds(k * 64 + 2 * c + half, 8, stride=8), :] = total[k * 8 : k * 8 + 8, half * 128 : half * 128 + 128]
        return carry

    lax.fori_loop(0, 4, columns, 0)

    row = lax.broadcasted_iota(i32, (8, 128), 0) & 3
    here_p = pres[...]
    above = jnp.where(row < 3, pltpu.roll(here_p, 7, 0), pltpu.roll(pres_after[...], 3, 0))
    below = jnp.where(row >= 1, pltpu.roll(here_p, 1, 0), pltpu.roll(pres_before[...], 5, 0))
    gradient = (above - below) / (2.0 * rho[...])
    gas = [vel[d] for d in range(3)]
    target = [gas[0] - gradient, gas[1], gas[2]]

    for k in range(LOCAL):
        half = 0.5 * source[k * 8 : k * 8 + 8, :]
        density = out[0, k] + half
        s = jnp.full((8, 128), stop[k], f32)
        share = 1.0 / (1.0 + s)
        pull = s * density
        out[0, k] = density
        for d in range(3):
            grown = out[d + 1, k] + half * gas[d]
            out[d + 1, k] = (grown + pull * target[d]) * share

    for copy in (*sends, relay0, relay1):
        copy.wait_send()
    for part in range(3):
        @pl.when(has_after)
        def _():
            ups[part].wait_send()

        @pl.when(has_before)
        def _():
            downs[part].wait_send()


VMEM_SPEC = pl.BlockSpec(memory_space=pltpu.VMEM)
SMEM_SPEC = pl.BlockSpec(memory_space=pltpu.SMEM)
ANY_SPEC = pl.BlockSpec(memory_space=pl.ANY)


def folded(value):
    lead = value.shape[:-2]
    value = value.reshape(*lead, 4, 2, 128)
    return jnp.swapaxes(value, -3, -2).reshape(*lead, 8, 128)


def unfolded(value):
    lead = value.shape[:-2]
    value = value.reshape(*lead, 2, 4, 128)
    return jnp.swapaxes(value, -3, -2).reshape(*lead, 4, 256)


def local(dust_state, drift_speed, stop_ratio, gas_rho, gas_vel, pressure, pair_list, outcome):
    rates = pl.pallas_call(
        sort_kernel,
        out_shape=jax.ShapeDtypeStruct((BINS * 32, 128), bf16),
        in_specs=[VMEM_SPEC, VMEM_SPEC],
        out_specs=VMEM_SPEC,
        scratch_shapes=[
            pltpu.VMEM((PADDED, 128), f32),
            pltpu.VMEM((128, 128), f32),
            pltpu.VMEM((128, 128), f32),
            pltpu.VMEM((BINS, 128), i32),
            pltpu.SMEM((BINS, 128), i32),
            pltpu.SemaphoreType.DMA,
        ],
        compiler_params=pltpu.CompilerParams(vmem_limit_bytes=24 << 20),
        name="sort_rates",
    )(outcome.T, pair_list.T)
    halo = pltpu.VMEM((4, LOCAL, 8, 128), f32)
    result = pl.pallas_call(
        step_kernel,
        out_shape=jax.ShapeDtypeStruct((4, LOCAL, 8, 128), f32),
        in_specs=[ANY_SPEC, SMEM_SPEC, SMEM_SPEC, VMEM_SPEC, VMEM_SPEC, VMEM_SPEC, VMEM_SPEC],
        out_specs=VMEM_SPEC,
        scratch_shapes=[
            halo, halo, halo,
            pltpu.VMEM((8, 128), f32),
            pltpu.VMEM((8, 128), f32),
            pltpu.VMEM((4 * 224, 128), f32),
            pltpu.VMEM((160, 1024), bf16),
            pltpu.VMEM((160, 1024), bf16),
            pltpu.VMEM((256, 128), f32),
            pltpu.SemaphoreType.DMA((2,)),
            pltpu.SemaphoreType.DMA((3,)),
            pltpu.SemaphoreType.DMA((3,)),
            pltpu.SemaphoreType.DMA((3,)),
            pltpu.SemaphoreType.DMA((3,)),
            pltpu.SemaphoreType.DMA((6,)),
            pltpu.SemaphoreType.DMA((6,)),
        ],
        compiler_params=pltpu.CompilerParams(
            collective_id=0, has_side_effects=True, vmem_limit_bytes=24 << 20
        ),
        name="dust_step",
    )(folded(dust_state), drift_speed, stop_ratio, folded(gas_rho), folded(gas_vel), folded(pressure), rates)
    return unfolded(result)


def solution(mesh):
    return jax.shard_map(
        local,
        mesh=mesh,
        in_specs=(
            P(None, "bins", "tiles", None),
            P("bins"),
            P("bins"),
            P("tiles", None),
            P(None, "tiles", None),
            P("tiles", None),
            P(),
            P(None, "bins"),
        ),
        out_specs=P(None, "bins", "tiles", None),
        check_vma=False,
    )
```

```python
import functools

import jax
import jax.numpy as jnp
from jax import lax
from jax.experimental import pallas as pl
from jax.experimental.pallas import tpu as pltpu
from jax.sharding import PartitionSpec as P

MESH = pl.DeviceIdType.MESH
BINS = 112
LOCAL = 28
PAIRS = 6328
GROUPS = 7
f32, bf16, i32 = jnp.float32, jnp.bfloat16, jnp.int32


def bin_at(group, member):
    if group < 6:
        tile = 2 * group + member // 8
        return tile // 3, (tile % 3) * 8 + member % 8
    return member // 4, 24 + member % 4


def group_member(index):
    shard = (index >= 28).astype(i32) + (index >= 56).astype(i32) + (index >= 84).astype(i32)
    own = index - 28 * shard
    tile = 3 * shard + (own >> 3)
    full = own < 24
    group = jnp.where(full, tile >> 1, 6)
    member = jnp.where(full, ((tile & 1) << 3) + (own & 7), 4 * shard + own - 24)
    return group, member


def slots_of(pairs):
    group_i, member_i = group_member(pairs[0:1, :])
    group_j, member_j = group_member(pairs[1:2, :])
    ahead = group_j - group_i
    ahead = jnp.where(ahead < 0, ahead + GROUPS, ahead)
    keep = ahead <= 3
    row = jnp.where(keep, group_i * 16 + member_i, group_j * 16 + member_j)
    slot = jnp.where(keep, ahead * 16 + member_j, (GROUPS - ahead) * 16 + member_i)
    return row, slot


def invert_pairs(pairs_ref, table_ref):
    total = jnp.zeros((BINS, 128), f32)
    for start in range(0, PAIRS, 256):
        width = min(256, PAIRS - start)
        row, slot = slots_of(pairs_ref[:, start : start + width])
        rows = lax.broadcasted_iota(i32, (BINS, width), 0)
        lanes = lax.broadcasted_iota(i32, (128, width), 0)
        number = start + 1 + lax.broadcasted_iota(i32, (1, width), 1)
        high = (number >> 6).astype(f32)
        low = (number & 63).astype(f32)
        value = jnp.where(lanes < 64, high, low)
        first = jnp.where(rows == row, 1.0, 0.0).astype(bf16)
        second = jnp.where((lanes & 63) == slot, value, 0.0).astype(bf16)
        total += lax.dot_general(first, second, (((1,), (1,)), ((), ())), preferred_element_type=f32)
    number = total * 64.0 + pltpu.roll(total, 64, 1)
    table_ref[...] = jnp.clip(number.astype(i32) - 1, 0, PAIRS - 1)


def turn_outcome(outcome_ref, turned_ref):
    for start in range(0, PAIRS, 128):
        width = min(128, PAIRS - start)
        turned_ref[start : start + width, 0:LOCAL] = outcome_ref[:, start : start + width].T


def gather_two(table, turned, held, two):
    for half in range(2):
        member = 2 * two + half
        for slot in range(member, 64):
            at = half * 64 + slot
            index = table[member % 8, slot]
            held[at : at + 1, :] = turned[pl.ds(index, 1), :]


def place_two(held, rates, group, two):
    lane = lax.broadcasted_iota(i32, (32, 128), 1)
    left = lane < 64
    unused = (lane < 2 * two) | ((lane >= 64) & (lane < 64 + 2 * two + 1))
    value = jnp.where(unused, 0.0, held[...].T[0:32, :])
    high = value.astype(bf16).astype(f32)
    low = pltpu.roll(value - high, 64, 1)
    start = pl.multiple_of(group * 512 + two * 64, 64)
    rates[pl.ds(start, 32), :] = jnp.where(left, high, low).astype(bf16)
    rates[pl.ds(start + 32, 32), :] = jnp.where(left, low, high).astype(bf16)


def sort_kernel(pairs_in, outcome_in, rates, pairs, outcome, turned, held, table_v, table_a, table_b, in_sem, table_sem):
    pairs_copy = pltpu.make_async_copy(pairs_in, pairs, in_sem.at[0])
    outcome_copy = pltpu.make_async_copy(outcome_in, outcome, in_sem.at[1])
    pairs_copy.start()
    outcome_copy.start()

    def table_copy(group, half):
        rows = pl.ds(pl.multiple_of(group * 16 + half * 8, 8), 8)
        return pltpu.make_async_copy(table_v.at[rows, :], (table_a, table_b)[half], table_sem.at[half])

    pairs_copy.wait()
    invert_pairs(pairs, table_v)
    table_copy(0, 0).start()
    table_copy(0, 1).start()
    outcome_copy.wait()
    turn_outcome(outcome, turned)

    def sort_group(group, carry):
        for half in range(2):
            table_copy(group, half).wait()
            for two in range(4 * half, 4 * half + 4):
                gather_two((table_a, table_b)[half], turned, held.at[two], two)
                place_two(held.at[two], rates, group, two)

            @pl.when(group < GROUPS - 1)
            def _():
                table_copy(jnp.minimum(group + 1, GROUPS - 1), half).start()

        return carry

    lax.fori_loop(0, GROUPS, sort_group, 0)


def transported(own, before, after, speed):
    forward = jnp.maximum(speed, 0.0)
    backward = jnp.maximum(-speed, 0.0)

    def weights(a):
        square = a * a
        return (2.0 * a - 3.0 * square, 2.75 * square - 0.5 * a, -square, 0.125 * square)

    a = forward + backward
    row = lax.broadcasted_iota(i32, (8, 128), 0) & 3
    result = (1.0 - 1.5 * a + 1.125 * (a * a)) * own
    up, down = weights(forward), weights(backward)
    for m in (1, 2, 3):
        result += up[m - 1] * jnp.where(row >= m, pltpu.roll(own, m, 0), pltpu.roll(before, 4 + m, 0))
        result += down[m - 1] * jnp.where(row < 4 - m, pltpu.roll(own, 8 - m, 0), pltpu.roll(after, 4 - m, 0))
    return result + up[3] * before + down[3] * after


def step_kernel(
    dust_in, speed, stop, rho, vel, pres, rates, out,
    own, before, after, pres_before, pres_after, dens, high, low, source,
    own_sem, up_send, up_recv, down_send, down_recv, ring_send, ring_recv,
):
    tile, shard = lax.axis_index("tiles"), lax.axis_index("bins")
    tiles, shards = lax.axis_size("tiles"), lax.axis_size("bins")
    has_before, has_after = tile > 0, tile < tiles - 1
    nxt, prv = lax.rem(shard + 1, shards), lax.rem(shard + shards - 1, shards)

    barrier = pltpu.get_barrier_semaphore()
    pl.semaphore_signal(barrier, inc=1, device_id={"bins": nxt}, device_id_type=MESH)
    pl.semaphore_signal(barrier, inc=1, device_id={"bins": prv}, device_id_type=MESH)

    @pl.when(has_before)
    def _():
        pl.semaphore_signal(barrier, inc=1, device_id={"tiles": tile - 1}, device_id_type=MESH)

    @pl.when(has_after)
    def _():
        pl.semaphore_signal(barrier, inc=1, device_id={"tiles": tile + 1}, device_id_type=MESH)

    own_copies = [
        pltpu.make_async_copy(dust_in.at[0:1], own.at[0:1], own_sem.at[0]),
        pltpu.make_async_copy(dust_in.at[1:4], own.at[1:4], own_sem.at[1]),
    ]
    own_copies[0].start()
    own_copies[1].start()

    pl.semaphore_wait(barrier, 2 + has_before.astype(i32) + has_after.astype(i32))

    def tile_copies(send, recv, target, there, pres_there):
        make = functools.partial(pltpu.make_async_remote_copy, device_id={"tiles": target}, device_id_type=MESH)
        return [
            make(dust_in.at[0:1], there.at[0:1], send.at[0], recv.at[0]),
            make(pres, pres_there, send.at[1], recv.at[1]),
            make(dust_in.at[1:4], there.at[1:4], send.at[2], recv.at[2]),
        ]

    ups = tile_copies(up_send, up_recv, tile + 1, before, pres_before)
    downs = tile_copies(down_send, down_recv, tile - 1, after, pres_after)

    for part in range(3):
        @pl.when(has_after)
        def _():
            ups[part].start()

        @pl.when(has_before)
        def _():
            downs[part].start()

    @pl.when(jnp.logical_not(has_before))
    def _():
        before[...] = jnp.zeros_like(before)
        pres_before[...] = jnp.zeros_like(pres_before)

    @pl.when(jnp.logical_not(has_after))
    def _():
        after[...] = jnp.zeros_like(after)
        pres_after[...] = jnp.zeros_like(pres_after)

    def arrived(part):
        @pl.when(has_before)
        def _():
            ups[part].wait_recv()

        @pl.when(has_after)
        def _():
            downs[part].wait_recv()

    own_copies[0].wait()
    arrived(0)
    here = shard * 224
    for k in range(LOCAL):
        moved = transported(own[0, k], before[0, k], after[0, k], jnp.full((8, 128), speed[k], f32))
        out[0, k] = moved
        dens[pl.ds(here + k, 8, stride=LOCAL), :] = moved

    def ring_copy(block, chunk, target, slot):
        piece = dens.at[pl.ds(pl.multiple_of(block * 224 + chunk * 56, 8), 56), :]
        return pltpu.make_async_remote_copy(
            piece, piece, ring_send.at[slot], ring_recv.at[slot],
            device_id={"bins": target}, device_id_type=MESH,
        )

    two_back = lax.rem(shard + 2, shards)
    forward, backward, relayed = (0, 1, 2, 3), (2, 3, 0, 1), (0, 2, 1, 3)
    sends = []
    for i in range(4):
        sends.append(ring_copy(shard, forward[i], nxt, forward[i]))
        sends.append(ring_copy(shard, backward[i], prv, 4 + backward[i]))
    for copy in sends:
        copy.start()
    from_prv = [ring_copy(prv, c, nxt, c) for c in range(4)]
    from_nxt = [ring_copy(nxt, c, prv, 4 + c) for c in range(4)]
    relays = [ring_copy(prv, c, nxt, 8 + c) if c < 2 else ring_copy(nxt, c, prv, 8 + c) for c in range(4)]
    far = [ring_copy(two_back, c, nxt if c < 2 else prv, 8 + c) for c in range(4)]

    def relay(c):
        (from_prv if c < 2 else from_nxt)[c].wait_recv()
        relays[c].start()

    def momenta(k, carry):
        rate = jnp.full((8, 128), speed[k], f32)
        for d in range(1, 4):
            out[d, k] = transported(own[d, k], before[d, k], after[d, k], rate)
        return carry

    relay(0)
    relay(2)
    own_copies[1].wait()
    arrived(1)
    arrived(2)
    lax.fori_loop(0, LOCAL, momenta, 0)
    relay(1)
    relay(3)

    for c in range(2):
        from_prv[2 + c].wait_recv()
        from_nxt[c].wait_recv()

    for c in relayed:
        far[c].wait_recv()
        for m in (2 * c, 2 * c + 1):
            for group in range(GROUPS):
                if group < 6:
                    starts = [bin_at(group, 0), bin_at(group, 8)]
                    pieces = [dens[b * 224 + m * 28 + w : b * 224 + m * 28 + w + 8, :] for b, w in starts]
                else:
                    pieces = [dens[b * 224 + m * 28 + 24 : b * 224 + m * 28 + 28, :] for b in range(4)]
                value = jnp.concatenate(pieces, 0)
                top = value.astype(bf16)
                rest = (value - top.astype(f32)).astype(bf16)
                for at in (group, group + GROUPS):
                    if at < 10:
                        high[at * 16 : at * 16 + 16, m * 128 : m * 128 + 128] = top
                        low[at * 16 : at * 16 + 16, m * 128 : m * 128 + 128] = rest
        total = jnp.zeros((32, 256), f32)
        for group in range(GROUPS):
            top = high[group * 16 : group * 16 + 64, c * 256 : c * 256 + 256]
            rest = low[group * 16 : group * 16 + 64, c * 256 : c * 256 + 256]
            weights = jnp.concatenate([top, top, rest, rest], 0)
            block = rates[group * 512 : group * 512 + 512, :]
            product = jnp.dot(jnp.concatenate([block, block], 1), weights, preferred_element_type=f32)
            for member in range(16):
                b, w = bin_at(group, member)
                start = b * 224 + w + c * 56
                line = jnp.concatenate([dens[start : start + 1, :], dens[start + 28 : start + 29, :]], 1)
                total += product[member * 32 : member * 32 + 32, :] * line
        for half in range(2):
            for k in range(4):
                source[pl.ds(k * 64 + 2 * c + half, 8, stride=8), :] = total[k * 8 : k * 8 + 8, half * 128 : half * 128 + 128]

    row = lax.broadcasted_iota(i32, (8, 128), 0) & 3
    here_p = pres[...]
    above = jnp.where(row < 3, pltpu.roll(here_p, 7, 0), pltpu.roll(pres_after[...], 3, 0))
    below = jnp.where(row >= 1, pltpu.roll(here_p, 1, 0), pltpu.roll(pres_before[...], 5, 0))
    gradient = (above - below) / (2.0 * rho[...])
    gas = [vel[d] for d in range(3)]
    target = [gas[0] - gradient, gas[1], gas[2]]

    for k in range(LOCAL):
        half = 0.5 * source[k * 8 : k * 8 + 8, :]
        density = out[0, k] + half
        s = jnp.full((8, 128), stop[k], f32)
        share = 1.0 / (1.0 + s)
        pull = s * density
        out[0, k] = density
        for d in range(3):
            grown = out[d + 1, k] + half * gas[d]
            out[d + 1, k] = (grown + pull * target[d]) * share

    for copy in (*sends, *relays):
        copy.wait_send()
    for part in range(3):
        @pl.when(has_after)
        def _():
            ups[part].wait_send()

        @pl.when(has_before)
        def _():
            downs[part].wait_send()


def folded(value):
    lead = value.shape[:-2]
    value = value.reshape(*lead, 4, 2, 128)
    return jnp.swapaxes(value, -3, -2).reshape(*lead, 8, 128)


def unfolded(value):
    lead = value.shape[:-2]
    value = value.reshape(*lead, 2, 4, 128)
    return jnp.swapaxes(value, -3, -2).reshape(*lead, 4, 256)


def local(dust_state, drift_speed, stop_ratio, gas_rho, gas_vel, pressure, pair_list, outcome):
    dma = pltpu.SemaphoreType.DMA
    in_hbm = pl.BlockSpec(memory_space=pltpu.HBM)
    in_vmem = pl.BlockSpec(memory_space=pltpu.VMEM)
    in_smem = pl.BlockSpec(memory_space=pltpu.SMEM)
    rates = pl.pallas_call(
        sort_kernel,
        out_shape=jax.ShapeDtypeStruct((BINS * 32, 128), bf16),
        in_specs=[in_hbm, in_hbm],
        out_specs=in_vmem,
        scratch_shapes=[
            pltpu.VMEM((2, PAIRS), i32),
            pltpu.VMEM((LOCAL, PAIRS), f32),
            pltpu.VMEM((PAIRS, 128), f32),
            pltpu.VMEM((8, 128, 128), f32),
            pltpu.VMEM((BINS, 128), i32),
            pltpu.SMEM((8, 128), i32),
            pltpu.SMEM((8, 128), i32),
            dma((2,)), dma((2,)),
        ],
        compiler_params=pltpu.CompilerParams(vmem_limit_bytes=24 << 20),
        name="sort_rates",
    )(pair_list.T, outcome.T)
    halo = pltpu.VMEM((4, LOCAL, 8, 128), f32)
    cell = pltpu.VMEM((8, 128), f32)
    result = pl.pallas_call(
        step_kernel,
        out_shape=jax.ShapeDtypeStruct((4, LOCAL, 8, 128), f32),
        in_specs=[pl.BlockSpec(memory_space=pl.ANY), in_smem, in_smem, in_vmem, in_vmem, in_vmem, in_vmem],
        out_specs=in_vmem,
        scratch_shapes=[
            halo, halo, halo, cell, cell,
            pltpu.VMEM((4 * 224, 128), f32),
            pltpu.VMEM((160, 1024), bf16),
            pltpu.VMEM((160, 1024), bf16),
            pltpu.VMEM((256, 128), f32),
            dma((2,)), dma((3,)), dma((3,)), dma((3,)), dma((3,)),
            dma((12,)), dma((12,)),
        ],
        compiler_params=pltpu.CompilerParams(collective_id=0, has_side_effects=True, vmem_limit_bytes=24 << 20),
        name="dust_step",
    )(folded(dust_state), drift_speed, stop_ratio, folded(gas_rho), folded(gas_vel), folded(pressure), rates)
    return unfolded(result)


def solution(mesh):
    return jax.shard_map(
        local,
        mesh=mesh,
        in_specs=(
            P(None, "bins", "tiles", None),
            P("bins"),
            P("bins"),
            P("tiles", None),
            P(None, "tiles", None),
            P("tiles", None),
            P(),
            P(None, "bins"),
        ),
        out_specs=P(None, "bins", "tiles", None),
        check_vma=False,
    )
```

```python
import functools

import jax
import jax.numpy as jnp
from jax import lax
from jax.experimental import pallas as pl
from jax.experimental.pallas import tpu as pltpu
from jax.sharding import PartitionSpec as P

MESH = pl.DeviceIdType.MESH
BINS = 112
LOCAL = 28
PAIRS = 6328
GROUPS = 7
f32, bf16, i32 = jnp.float32, jnp.bfloat16, jnp.int32


def bin_at(group, member):
    if group < 6:
        tile = 2 * group + member // 8
        return tile // 3, (tile % 3) * 8 + member % 8
    return member // 4, 24 + member % 4


def group_member(index):
    shard = (index >= 28).astype(i32) + (index >= 56).astype(i32) + (index >= 84).astype(i32)
    own = index - 28 * shard
    tile = 3 * shard + (own >> 3)
    full = own < 24
    group = jnp.where(full, tile >> 1, 6)
    member = jnp.where(full, ((tile & 1) << 3) + (own & 7), 4 * shard + own - 24)
    return group, member


def slots_of(pairs):
    group_i, member_i = group_member(pairs[0:1, :])
    group_j, member_j = group_member(pairs[1:2, :])
    ahead = group_j - group_i
    ahead = jnp.where(ahead < 0, ahead + GROUPS, ahead)
    keep = ahead <= 3
    row = jnp.where(keep, group_i * 16 + member_i, group_j * 16 + member_j)
    slot = jnp.where(keep, ahead * 16 + member_j, (GROUPS - ahead) * 16 + member_i)
    return row, slot


def invert_pairs(pairs_ref, table_ref):
    total = jnp.zeros((BINS, 128), f32)
    for start in range(0, PAIRS, 256):
        width = min(256, PAIRS - start)
        row, slot = slots_of(pairs_ref[:, start : start + width])
        rows = lax.broadcasted_iota(i32, (BINS, width), 0)
        lanes = lax.broadcasted_iota(i32, (128, width), 0)
        number = start + 1 + lax.broadcasted_iota(i32, (1, width), 1)
        high = (number >> 6).astype(f32)
        low = (number & 63).astype(f32)
        value = jnp.where(lanes < 64, high, low)
        first = jnp.where(rows == row, 1.0, 0.0).astype(bf16)
        second = jnp.where((lanes & 63) == slot, value, 0.0).astype(bf16)
        total += lax.dot_general(first, second, (((1,), (1,)), ((), ())), preferred_element_type=f32)
    number = total * 64.0 + pltpu.roll(total, 64, 1)
    table_ref[...] = jnp.clip(number.astype(i32) - 1, 0, PAIRS - 1)


def turn_outcome(outcome_ref, turned_ref):
    for start in range(0, PAIRS, 128):
        width = min(128, PAIRS - start)
        turned_ref[start : start + width, 0:LOCAL] = outcome_ref[:, start : start + width].T


def gather_two(table, turned, held, two):
    for half in range(2):
        member = 2 * two + half
        for slot in range(member, 64):
            at = half * 64 + slot
            index = table[member % 8, slot]
            held[at : at + 1, :] = turned[pl.ds(index, 1), :]


def place_two(held, rates, group, two):
    lane = lax.broadcasted_iota(i32, (32, 128), 1)
    left = lane < 64
    unused = (lane < 2 * two) | ((lane >= 64) & (lane < 64 + 2 * two + 1))
    value = jnp.where(unused, 0.0, held[...].T[0:32, :])
    high = value.astype(bf16).astype(f32)
    low = pltpu.roll(value - high, 64, 1)
    start = pl.multiple_of(group * 512 + two * 64, 64)
    rates[pl.ds(start, 32), :] = jnp.where(left, high, low).astype(bf16)
    rates[pl.ds(start + 32, 32), :] = jnp.where(left, low, high).astype(bf16)


def transported(own, before, after, speed):
    forward = jnp.maximum(speed, 0.0)
    backward = jnp.maximum(-speed, 0.0)

    def weights(a):
        square = a * a
        return (2.0 * a - 3.0 * square, 2.75 * square - 0.5 * a, -square, 0.125 * square)

    a = forward + backward
    row = lax.broadcasted_iota(i32, (8, 128), 0) & 3
    result = (1.0 - 1.5 * a + 1.125 * (a * a)) * own
    up, down = weights(forward), weights(backward)
    for m in (1, 2, 3):
        result += up[m - 1] * jnp.where(row >= m, pltpu.roll(own, m, 0), pltpu.roll(before, 4 + m, 0))
        result += down[m - 1] * jnp.where(row < 4 - m, pltpu.roll(own, 8 - m, 0), pltpu.roll(after, 4 - m, 0))
    return result + up[3] * before + down[3] * after


def step_kernel(
    dust_in, speed_in, stop_in, rho_in, vel_in, pres_in, pairs_in, outcome_in, out,
    own, before, after, pres_before, pres_after, dens, high, low, source,
    speed, stop, rho, vel, pres, pairs, outcome,
    turned, held, table_v, table_a, table_b, rates,
    own_sem, in_sem, table_sem, up_send, up_recv, down_send, down_recv, ring_send, ring_recv,
):
    tile, shard = lax.axis_index("tiles"), lax.axis_index("bins")
    tiles, shards = lax.axis_size("tiles"), lax.axis_size("bins")
    has_before, has_after = tile > 0, tile < tiles - 1
    nxt, prv = lax.rem(shard + 1, shards), lax.rem(shard + shards - 1, shards)

    barrier = pltpu.get_barrier_semaphore()
    pl.semaphore_signal(barrier, inc=1, device_id={"bins": nxt}, device_id_type=MESH)
    pl.semaphore_signal(barrier, inc=1, device_id={"bins": prv}, device_id_type=MESH)

    @pl.when(has_before)
    def _():
        pl.semaphore_signal(barrier, inc=1, device_id={"tiles": tile - 1}, device_id_type=MESH)

    @pl.when(has_after)
    def _():
        pl.semaphore_signal(barrier, inc=1, device_id={"tiles": tile + 1}, device_id_type=MESH)

    own_copies = [
        pltpu.make_async_copy(dust_in.at[0:1], own.at[0:1], own_sem.at[0]),
        pltpu.make_async_copy(dust_in.at[1:4], own.at[1:4], own_sem.at[1]),
    ]
    moves = ((pairs_in, pairs), (speed_in, speed), (outcome_in, outcome), (stop_in, stop), (rho_in, rho), (vel_in, vel), (pres_in, pres))
    pairs_copy, speed_copy, outcome_copy, *late_copies = [
        pltpu.make_async_copy(source_ref, target_ref, in_sem.at[i]) for i, (source_ref, target_ref) in enumerate(moves)
    ]
    pairs_copy.start()
    own_copies[0].start()
    speed_copy.start()
    outcome_copy.start()
    own_copies[1].start()
    for copy in late_copies:
        copy.start()

    pl.semaphore_wait(barrier, 2 + has_before.astype(i32) + has_after.astype(i32))

    def tile_copies(send, recv, target, there, pres_there):
        make = functools.partial(pltpu.make_async_remote_copy, device_id={"tiles": target}, device_id_type=MESH)
        return [
            make(dust_in.at[0:1], there.at[0:1], send.at[0], recv.at[0]),
            make(pres_in, pres_there, send.at[1], recv.at[1]),
            make(dust_in.at[1:4], there.at[1:4], send.at[2], recv.at[2]),
        ]

    ups = tile_copies(up_send, up_recv, tile + 1, before, pres_before)
    downs = tile_copies(down_send, down_recv, tile - 1, after, pres_after)

    for part in range(3):
        @pl.when(has_after)
        def _():
            ups[part].start()

        @pl.when(has_before)
        def _():
            downs[part].start()

    @pl.when(jnp.logical_not(has_before))
    def _():
        before[...] = jnp.zeros_like(before)
        pres_before[...] = jnp.zeros_like(pres_before)

    @pl.when(jnp.logical_not(has_after))
    def _():
        after[...] = jnp.zeros_like(after)
        pres_after[...] = jnp.zeros_like(pres_after)

    def arrived(part):
        @pl.when(has_before)
        def _():
            ups[part].wait_recv()

        @pl.when(has_after)
        def _():
            downs[part].wait_recv()

    pairs_copy.wait()
    invert_pairs(pairs, table_v)

    def table_copy(group, half):
        rows = pl.ds(pl.multiple_of(group * 16 + half * 8, 8), 8)
        return pltpu.make_async_copy(table_v.at[rows, :], (table_a, table_b)[half], table_sem.at[half])

    table_copy(0, 0).start()
    table_copy(0, 1).start()
    outcome_copy.wait()
    turn_outcome(outcome, turned)

    own_copies[0].wait()
    speed_copy.wait()
    arrived(0)
    here = shard * 224
    for k in range(LOCAL):
        moved = transported(own[0, k], before[0, k], after[0, k], jnp.full((8, 128), speed[k], f32))
        out[0, k] = moved
        dens[pl.ds(here + k, 8, stride=LOCAL), :] = moved

    def ring_copy(block, chunk, target, slot):
        piece = dens.at[pl.ds(pl.multiple_of(block * 224 + chunk * 56, 8), 56), :]
        return pltpu.make_async_remote_copy(
            piece, piece, ring_send.at[slot], ring_recv.at[slot],
            device_id={"bins": target}, device_id_type=MESH,
        )

    two_back = lax.rem(shard + 2, shards)
    forward, backward, relayed = (0, 1, 2, 3), (2, 3, 0, 1), (0, 2, 1, 3)
    sends = []
    for i in range(4):
        sends.append(ring_copy(shard, forward[i], nxt, forward[i]))
        sends.append(ring_copy(shard, backward[i], prv, 4 + backward[i]))
    for copy in sends:
        copy.start()
    from_prv = [ring_copy(prv, c, nxt, c) for c in range(4)]
    from_nxt = [ring_copy(nxt, c, prv, 4 + c) for c in range(4)]
    relays = [ring_copy(prv, c, nxt, 8 + c) if c < 2 else ring_copy(nxt, c, prv, 8 + c) for c in range(4)]
    far = [ring_copy(two_back, c, nxt if c < 2 else prv, 8 + c) for c in range(4)]

    def sort_group(group, carry):
        for half in range(2):
            table_copy(group, half).wait()
            for two in range(4 * half, 4 * half + 4):
                gather_two((table_a, table_b)[half], turned, held.at[two], two)
                if two > 0:
                    place_two(held.at[two - 1], rates, group, two - 1)
                else:
                    place_two(held.at[7], rates, jnp.maximum(group - 1, 0), 7)

            @pl.when(group < GROUPS - 1)
            def _():
                table_copy(jnp.minimum(group + 1, GROUPS - 1), half).start()

        return carry

    def relay(c):
        (from_prv if c < 2 else from_nxt)[c].wait_recv()
        relays[c].start()

    lax.fori_loop(0, 4, sort_group, 0)
    relay(0)
    relay(2)
    lax.fori_loop(4, 6, sort_group, 0)
    relay(1)
    relay(3)
    lax.fori_loop(6, GROUPS, sort_group, 0)
    place_two(held.at[7], rates, GROUPS - 1, 7)

    own_copies[1].wait()
    arrived(1)
    arrived(2)

    def momenta(k, carry):
        rate = jnp.full((8, 128), speed[k], f32)
        for d in range(1, 4):
            out[d, k] = transported(own[d, k], before[d, k], after[d, k], rate)
        return carry

    lax.fori_loop(0, LOCAL, momenta, 0)

    for c in range(2):
        from_prv[2 + c].wait_recv()
        from_nxt[c].wait_recv()

    for c in relayed:
        far[c].wait_recv()
        for m in (2 * c, 2 * c + 1):
            for group in range(GROUPS):
                if group < 6:
                    starts = [bin_at(group, 0), bin_at(group, 8)]
                    pieces = [dens[b * 224 + m * 28 + w : b * 224 + m * 28 + w + 8, :] for b, w in starts]
                else:
                    pieces = [dens[b * 224 + m * 28 + 24 : b * 224 + m * 28 + 28, :] for b in range(4)]
                value = jnp.concatenate(pieces, 0)
                top = value.astype(bf16)
                rest = (value - top.astype(f32)).astype(bf16)
                for at in (group, group + GROUPS):
                    if at < 10:
                        high[at * 16 : at * 16 + 16, m * 128 : m * 128 + 128] = top
                        low[at * 16 : at * 16 + 16, m * 128 : m * 128 + 128] = rest
        total = jnp.zeros((32, 256), f32)
        for group in range(GROUPS):
            top = high[group * 16 : group * 16 + 64, c * 256 : c * 256 + 256]
            rest = low[group * 16 : group * 16 + 64, c * 256 : c * 256 + 256]
            weights = jnp.concatenate([top, top, rest, rest], 0)
            block = rates[group * 512 : group * 512 + 512, :]
            product = jnp.dot(jnp.concatenate([block, block], 1), weights, preferred_element_type=f32)
            for member in range(16):
                b, w = bin_at(group, member)
                start = b * 224 + w + c * 56
                line = jnp.concatenate([dens[start : start + 1, :], dens[start + 28 : start + 29, :]], 1)
                total += product[member * 32 : member * 32 + 32, :] * line
        for half in range(2):
            for k in range(4):
                source[pl.ds(k * 64 + 2 * c + half, 8, stride=8), :] = total[k * 8 : k * 8 + 8, half * 128 : half * 128 + 128]

    for copy in late_copies:
        copy.wait()
    row = lax.broadcasted_iota(i32, (8, 128), 0) & 3
    here_p = pres[...]
    above = jnp.where(row < 3, pltpu.roll(here_p, 7, 0), pltpu.roll(pres_after[...], 3, 0))
    below = jnp.where(row >= 1, pltpu.roll(here_p, 1, 0), pltpu.roll(pres_before[...], 5, 0))
    gradient = (above - below) / (2.0 * rho[...])
    gas = [vel[d] for d in range(3)]
    target = [gas[0] - gradient, gas[1], gas[2]]

    for k in range(LOCAL):
        half = 0.5 * source[k * 8 : k * 8 + 8, :]
        density = out[0, k] + half
        s = jnp.full((8, 128), stop[k], f32)
        share = 1.0 / (1.0 + s)
        pull = s * density
        out[0, k] = density
        for d in range(3):
            grown = out[d + 1, k] + half * gas[d]
            out[d + 1, k] = (grown + pull * target[d]) * share

    for copy in (*sends, *relays):
        copy.wait_send()
    for part in range(3):
        @pl.when(has_after)
        def _():
            ups[part].wait_send()

        @pl.when(has_before)
        def _():
            downs[part].wait_send()


def folded(value):
    lead = value.shape[:-2]
    value = value.reshape(*lead, 4, 2, 128)
    return jnp.swapaxes(value, -3, -2).reshape(*lead, 8, 128)


def unfolded(value):
    lead = value.shape[:-2]
    value = value.reshape(*lead, 2, 4, 128)
    return jnp.swapaxes(value, -3, -2).reshape(*lead, 4, 256)


def local(dust_state, drift_speed, stop_ratio, gas_rho, gas_vel, pressure, pair_list, outcome):
    halo = pltpu.VMEM((4, LOCAL, 8, 128), f32)
    cell = pltpu.VMEM((8, 128), f32)
    dma = pltpu.SemaphoreType.DMA
    result = pl.pallas_call(
        step_kernel,
        out_shape=jax.ShapeDtypeStruct((4, LOCAL, 8, 128), f32),
        in_specs=[pl.BlockSpec(memory_space=pl.ANY)] * 8,
        out_specs=pl.BlockSpec(memory_space=pltpu.VMEM),
        scratch_shapes=[
            halo, halo, halo, cell, cell,
            pltpu.VMEM((4 * 224, 128), f32),
            pltpu.VMEM((160, 1024), bf16),
            pltpu.VMEM((160, 1024), bf16),
            pltpu.VMEM((256, 128), f32),
            pltpu.SMEM((LOCAL,), f32),
            pltpu.SMEM((LOCAL,), f32),
            cell,
            pltpu.VMEM((3, 8, 128), f32),
            cell,
            pltpu.VMEM((2, PAIRS), i32),
            pltpu.VMEM((LOCAL, PAIRS), f32),
            pltpu.VMEM((PAIRS, 128), f32),
            pltpu.VMEM((8, 128, 128), f32),
            pltpu.VMEM((BINS, 128), i32),
            pltpu.SMEM((8, 128), i32),
            pltpu.SMEM((8, 128), i32),
            pltpu.VMEM((BINS * 32, 128), bf16),
            dma((2,)), dma((7,)), dma((2,)),
            dma((3,)), dma((3,)), dma((3,)), dma((3,)),
            dma((12,)), dma((12,)),
        ],
        compiler_params=pltpu.CompilerParams(collective_id=0, has_side_effects=True),
        name="dust_step",
    )(
        folded(dust_state), drift_speed, stop_ratio, folded(gas_rho), folded(gas_vel), folded(pressure),
        pair_list.T, outcome.T,
    )
    return unfolded(result)


def solution(mesh):
    return jax.shard_map(
        local,
        mesh=mesh,
        in_specs=(
            P(None, "bins", "tiles", None),
            P("bins"),
            P("bins"),
            P("tiles", None),
            P(None, "tiles", None),
            P("tiles", None),
            P(),
            P(None, "bins"),
        ),
        out_specs=P(None, "bins", "tiles", None),
        check_vma=False,
    )
```

```python
import functools

import jax
import jax.numpy as jnp
from jax import lax
from jax.experimental import pallas as pl
from jax.experimental.pallas import tpu as pltpu
from jax.sharding import PartitionSpec as P

MESH = pl.DeviceIdType.MESH
BINS = 112
LOCAL = 28
PAIRS = 6328
HALF = BINS // 2
UNITS = 7
GROUPS = 7
f32, bf16, i32 = jnp.float32, jnp.bfloat16, jnp.int32


def bin_at(group, member):
    if group < 6:
        tile = 2 * group + member // 8
        return tile // 3, (tile % 3) * 8 + member % 8
    return member // 4, 24 + member % 4


def group_member(index):
    shard = (index >= 28).astype(i32) + (index >= 56).astype(i32) + (index >= 84).astype(i32)
    own = index - 28 * shard
    tile = 3 * shard + (own >> 3)
    full = own < 24
    group = jnp.where(full, tile >> 1, 6)
    member = jnp.where(full, ((tile & 1) << 3) + (own & 7), 4 * shard + own - 24)
    return group, member


def slots_of(pairs):
    group_i, member_i = group_member(pairs[0:1, :])
    group_j, member_j = group_member(pairs[1:2, :])
    ahead = group_j - group_i
    ahead = jnp.where(ahead < 0, ahead + GROUPS, ahead)
    keep = ahead <= 3
    row = jnp.where(keep, group_i * 16 + member_i, group_j * 16 + member_j)
    slot = jnp.where(keep, ahead * 16 + member_j, (GROUPS - ahead) * 16 + member_i)
    return row, slot


def invert_pairs(pairs_ref, table_ref, core):
    total = jnp.zeros((HALF, 128), f32)
    for start in range(0, PAIRS, 256):
        width = min(256, PAIRS - start)
        row, slot = slots_of(pairs_ref[:, start : start + width])
        rows = lax.broadcasted_iota(i32, (HALF, width), 0)
        lanes = lax.broadcasted_iota(i32, (128, width), 0)
        number = start + 1 + lax.broadcasted_iota(i32, (1, width), 1)
        high = (number >> 6).astype(f32)
        low = (number & 63).astype(f32)
        value = jnp.where(lanes < 64, high, low)
        first = jnp.where(rows == row - HALF * core, 1.0, 0.0).astype(bf16)
        second = jnp.where((lanes & 63) == slot, value, 0.0).astype(bf16)
        total += lax.dot_general(first, second, (((1,), (1,)), ((), ())), preferred_element_type=f32)
    number = total * 64.0 + pltpu.roll(total, 64, 1)
    table_ref[...] = jnp.clip(number.astype(i32) - 1, 0, PAIRS - 1)


def turn_outcome(outcome_ref, turned_ref):
    for start in range(0, PAIRS, 128):
        width = min(128, PAIRS - start)
        turned_ref[start : start + width, 0:LOCAL] = outcome_ref[:, start : start + width].T


def gather_two(table, turned, held, two):
    for half in range(2):
        member = 2 * two + half
        for slot in range(member, 64):
            at = half * 64 + slot
            index = table[member, slot]
            held[at : at + 1, :] = turned[pl.ds(index, 1), :]


def place_two(value, rates, unit, two):
    lane = lax.broadcasted_iota(i32, (32, 128), 1)
    left = lane < 64
    member = lax.rem(unit, 2) * 8 + 2 * two
    value = jnp.where((lane & 63) < jnp.where(left, member, member + 1), 0.0, value)
    high = value.astype(bf16).astype(f32)
    low = pltpu.roll(value - high, 64, 1)
    start = pl.multiple_of(unit * 256 + two * 64, 64)
    rates[pl.ds(start, 32), :] = jnp.where(left, high, low).astype(bf16)
    rates[pl.ds(start + 32, 32), :] = jnp.where(left, low, high).astype(bf16)


def transported(own, before, after, speed):
    forward = jnp.maximum(speed, 0.0)
    backward = jnp.maximum(-speed, 0.0)

    def weights(a):
        square = a * a
        return (2.0 * a - 3.0 * square, 2.75 * square - 0.5 * a, -square, 0.125 * square)

    a = forward + backward
    row = lax.broadcasted_iota(i32, (8, 128), 0) & 3
    result = (1.0 - 1.5 * a + 1.125 * (a * a)) * own
    up, down = weights(forward), weights(backward)
    for m in (1, 2, 3):
        result += up[m - 1] * jnp.where(row >= m, pltpu.roll(own, m, 0), pltpu.roll(before, 4 + m, 0))
        result += down[m - 1] * jnp.where(row < 4 - m, pltpu.roll(own, 8 - m, 0), pltpu.roll(after, 4 - m, 0))
    return result + up[3] * before + down[3] * after


def step_kernel(
    dust_in, speed_in, stop_in, rho_in, vel_in, pres_in, pairs_in, outcome_in, out,
    own, before, after, pres_before, pres_after, dens, high, low, source,
    speed, stop, rho, vel, pres, pairs, outcome,
    turned, held, turns, table_v, table_a, table_b, rates,
    own_sem, in_sem, table_sem, up_send, up_recv, down_send, down_recv, ring_send, ring_recv, turn_send, turn_recv,
):
    tile, shard = lax.axis_index("tiles"), lax.axis_index("bins")
    tiles, shards = lax.axis_size("tiles"), lax.axis_size("bins")
    has_before, has_after = tile > 0, tile < tiles - 1
    core = lax.rem(tile, 2)
    nxt, prv = lax.rem(shard + 1, shards), lax.rem(shard + shards - 1, shards)

    barrier = pltpu.get_barrier_semaphore()
    pl.semaphore_signal(barrier, inc=1, device_id={"bins": nxt}, device_id_type=MESH)
    pl.semaphore_signal(barrier, inc=1, device_id={"bins": prv}, device_id_type=MESH)

    @pl.when(has_before)
    def _():
        pl.semaphore_signal(barrier, inc=1, device_id={"tiles": tile - 1}, device_id_type=MESH)

    @pl.when(has_after)
    def _():
        pl.semaphore_signal(barrier, inc=1, device_id={"tiles": tile + 1}, device_id_type=MESH)

    own_copies = [
        pltpu.make_async_copy(dust_in.at[0:1], own.at[0:1], own_sem.at[0]),
        pltpu.make_async_copy(dust_in.at[1:4], own.at[1:4], own_sem.at[1]),
    ]
    moves = ((pairs_in, pairs), (speed_in, speed), (outcome_in, outcome), (stop_in, stop), (rho_in, rho), (vel_in, vel), (pres_in, pres))
    pairs_copy, speed_copy, outcome_copy, *late_copies = [
        pltpu.make_async_copy(source_ref, target_ref, in_sem.at[i]) for i, (source_ref, target_ref) in enumerate(moves)
    ]
    pairs_copy.start()
    own_copies[0].start()
    speed_copy.start()
    outcome_copy.start()
    own_copies[1].start()
    for copy in late_copies:
        copy.start()

    pl.semaphore_wait(barrier, 2 + has_before.astype(i32) + has_after.astype(i32))

    def tile_copies(send, recv, target, there, pres_there):
        make = functools.partial(pltpu.make_async_remote_copy, device_id={"tiles": target}, device_id_type=MESH)
        return [
            make(dust_in.at[0:1], there.at[0:1], send.at[0], recv.at[0]),
            make(pres_in, pres_there, send.at[1], recv.at[1]),
            make(dust_in.at[1:4], there.at[1:4], send.at[2], recv.at[2]),
        ]

    ups = tile_copies(up_send, up_recv, tile + 1, before, pres_before)
    downs = tile_copies(down_send, down_recv, tile - 1, after, pres_after)

    for part in range(3):
        @pl.when(has_after)
        def _():
            ups[part].start()

        @pl.when(has_before)
        def _():
            downs[part].start()

    @pl.when(jnp.logical_not(has_before))
    def _():
        before[...] = jnp.zeros_like(before)
        pres_before[...] = jnp.zeros_like(pres_before)

    @pl.when(jnp.logical_not(has_after))
    def _():
        after[...] = jnp.zeros_like(after)
        pres_after[...] = jnp.zeros_like(pres_after)

    def arrived(part):
        @pl.when(has_before)
        def _():
            ups[part].wait_recv()

        @pl.when(has_after)
        def _():
            downs[part].wait_recv()

    pairs_copy.wait()
    invert_pairs(pairs, table_v, core)

    tables = (table_a, table_b)

    def table_copy(unit):
        return pltpu.make_async_copy(table_v.at[8 * unit : 8 * unit + 8, :], tables[unit % 2], table_sem.at[unit % 2])

    table_copy(0).start()
    table_copy(1).start()
    outcome_copy.wait()
    turn_outcome(outcome, turned)

    own_copies[0].wait()
    speed_copy.wait()
    arrived(0)
    here = shard * 224
    for k in range(LOCAL):
        moved = transported(own[0, k], before[0, k], after[0, k], jnp.full((8, 128), speed[k], f32))
        out[0, k] = moved
        dens[pl.ds(here + k, 8, stride=LOCAL), :] = moved

    def ring_copy(block, chunk, target, slot):
        piece = dens.at[pl.ds(pl.multiple_of(block * 224 + chunk * 56, 8), 56), :]
        return pltpu.make_async_remote_copy(
            piece, piece, ring_send.at[slot], ring_recv.at[slot],
            device_id={"bins": target}, device_id_type=MESH,
        )

    two_back = lax.rem(shard + 2, shards)
    forward, backward, relayed = (0, 1, 2, 3), (2, 3, 0, 1), (0, 2, 1, 3)
    sends = []
    for i in range(4):
        sends.append(ring_copy(shard, forward[i], nxt, forward[i]))
        sends.append(ring_copy(shard, backward[i], prv, 4 + backward[i]))
    for copy in sends:
        copy.start()
    from_prv = [ring_copy(prv, c, nxt, c) for c in range(4)]
    from_nxt = [ring_copy(nxt, c, prv, 4 + c) for c in range(4)]
    relays = [ring_copy(prv, c, nxt, 8 + c) if c < 2 else ring_copy(nxt, c, prv, 8 + c) for c in range(4)]
    far = [ring_copy(two_back, c, nxt if c < 2 else prv, 8 + c) for c in range(4)]

    first_unit = core * UNITS
    other_unit = UNITS - first_unit

    def turn_copy(unit):
        piece = turns.at[pl.ds((first_unit + unit) * 4, 4)]
        return pltpu.make_async_remote_copy(
            piece, piece, turn_send.at[unit], turn_recv.at[unit],
            device_id={"tiles": tile + 1 - 2 * core}, device_id_type=MESH,
        )

    def arriving(unit):
        piece = turns.at[pl.ds((other_unit + unit) * 4, 4)]
        return pltpu.make_async_remote_copy(
            piece, piece, turn_send.at[unit], turn_recv.at[unit],
            device_id={"tiles": tile + 1 - 2 * core}, device_id_type=MESH,
        )

    def finish(unit, two):
        value = held[(unit % 2) * 4 + two].T[0:32, :]
        turns[(first_unit + unit) * 4 + two] = value
        place_two(value, rates, first_unit + unit, two)

    def sort_unit(unit):
        table_copy(unit).wait()
        for two in range(4):
            gather_two(tables[unit % 2], turned, held.at[(unit % 2) * 4 + two], two)
            if two > 0:
                finish(unit, two - 1)
            elif unit > 0:
                finish(unit - 1, 3)
        if unit > 0:
            turn_copy(unit - 1).start()
        if unit + 2 < UNITS:
            table_copy(unit + 2).start()

    def relay(c):
        (from_prv if c < 2 else from_nxt)[c].wait_recv()
        relays[c].start()

    for unit in range(6):
        sort_unit(unit)
    relay(0)
    relay(2)
    sort_unit(6)
    finish(6, 3)

    own_copies[1].wait()
    arrived(1)
    arrived(2)
    turn_copy(6).start()

    def momenta(k, carry):
        rate = jnp.full((8, 128), speed[k], f32)
        for d in range(1, 4):
            out[d, k] = transported(own[d, k], before[d, k], after[d, k], rate)
        return carry

    lax.fori_loop(0, LOCAL, momenta, 0)
    relay(1)
    relay(3)

    for unit in range(UNITS):
        arriving(unit).wait_recv()

    def place_unit(unit, carry):
        for two in range(4):
            place_two(turns[(other_unit + unit) * 4 + two], rates, other_unit + unit, two)
        return carry

    lax.fori_loop(0, UNITS, place_unit, 0)

    for c in range(2):
        from_prv[2 + c].wait_recv()
        from_nxt[c].wait_recv()

    for c in relayed:
        far[c].wait_recv()
        for m in (2 * c, 2 * c + 1):
            for group in range(GROUPS):
                if group < 6:
                    starts = [bin_at(group, 0), bin_at(group, 8)]
                    pieces = [dens[b * 224 + m * 28 + w : b * 224 + m * 28 + w + 8, :] for b, w in starts]
                else:
                    pieces = [dens[b * 224 + m * 28 + 24 : b * 224 + m * 28 + 28, :] for b in range(4)]
                value = jnp.concatenate(pieces, 0)
                top = value.astype(bf16)
                rest = (value - top.astype(f32)).astype(bf16)
                for at in (group, group + GROUPS):
                    if at < 10:
                        high[at * 16 : at * 16 + 16, m * 128 : m * 128 + 128] = top
                        low[at * 16 : at * 16 + 16, m * 128 : m * 128 + 128] = rest
        total = jnp.zeros((32, 256), f32)
        for group in range(GROUPS):
            top = high[group * 16 : group * 16 + 64, c * 256 : c * 256 + 256]
            rest = low[group * 16 : group * 16 + 64, c * 256 : c * 256 + 256]
            weights = jnp.concatenate([top, top, rest, rest], 0)
            block = rates[group * 512 : group * 512 + 512, :]
            product = jnp.dot(jnp.concatenate([block, block], 1), weights, preferred_element_type=f32)
            for member in range(16):
                b, w = bin_at(group, member)
                start = b * 224 + w + c * 56
                line = jnp.concatenate([dens[start : start + 1, :], dens[start + 28 : start + 29, :]], 1)
                total += product[member * 32 : member * 32 + 32, :] * line
        for half in range(2):
            for k in range(4):
                source[pl.ds(k * 64 + 2 * c + half, 8, stride=8), :] = total[k * 8 : k * 8 + 8, half * 128 : half * 128 + 128]

    for copy in late_copies:
        copy.wait()
    row = lax.broadcasted_iota(i32, (8, 128), 0) & 3
    here_p = pres[...]
    above = jnp.where(row < 3, pltpu.roll(here_p, 7, 0), pltpu.roll(pres_after[...], 3, 0))
    below = jnp.where(row >= 1, pltpu.roll(here_p, 1, 0), pltpu.roll(pres_before[...], 5, 0))
    gradient = (above - below) / (2.0 * rho[...])
    gas = [vel[d] for d in range(3)]
    target = [gas[0] - gradient, gas[1], gas[2]]

    for k in range(LOCAL):
        half = 0.5 * source[k * 8 : k * 8 + 8, :]
        density = out[0, k] + half
        s = jnp.full((8, 128), stop[k], f32)
        share = 1.0 / (1.0 + s)
        pull = s * density
        out[0, k] = density
        for d in range(3):
            grown = out[d + 1, k] + half * gas[d]
            out[d + 1, k] = (grown + pull * target[d]) * share

    for copy in (*sends, *relays, *[turn_copy(unit) for unit in range(UNITS)]):
        copy.wait_send()
    for part in range(3):
        @pl.when(has_after)
        def _():
            ups[part].wait_send()

        @pl.when(has_before)
        def _():
            downs[part].wait_send()


def folded(value):
    lead = value.shape[:-2]
    value = value.reshape(*lead, 4, 2, 128)
    return jnp.swapaxes(value, -3, -2).reshape(*lead, 8, 128)


def unfolded(value):
    lead = value.shape[:-2]
    value = value.reshape(*lead, 2, 4, 128)
    return jnp.swapaxes(value, -3, -2).reshape(*lead, 4, 256)


def local(dust_state, drift_speed, stop_ratio, gas_rho, gas_vel, pressure, pair_list, outcome):
    halo = pltpu.VMEM((4, LOCAL, 8, 128), f32)
    cell = pltpu.VMEM((8, 128), f32)
    dma = pltpu.SemaphoreType.DMA
    result = pl.pallas_call(
        step_kernel,
        out_shape=jax.ShapeDtypeStruct((4, LOCAL, 8, 128), f32),
        in_specs=[pl.BlockSpec(memory_space=pl.ANY)] * 8,
        out_specs=pl.BlockSpec(memory_space=pltpu.VMEM),
        scratch_shapes=[
            halo, halo, halo, cell, cell,
            pltpu.VMEM((4 * 224, 128), f32),
            pltpu.VMEM((160, 1024), bf16),
            pltpu.VMEM((160, 1024), bf16),
            pltpu.VMEM((256, 128), f32),
            pltpu.SMEM((LOCAL,), f32),
            pltpu.SMEM((LOCAL,), f32),
            cell,
            pltpu.VMEM((3, 8, 128), f32),
            cell,
            pltpu.VMEM((2, PAIRS), i32),
            pltpu.VMEM((LOCAL, PAIRS), f32),
            pltpu.VMEM((PAIRS, 128), f32),
            pltpu.VMEM((8, 128, 128), f32),
            pltpu.VMEM((2 * UNITS * 4, 32, 128), f32),
            pltpu.VMEM((HALF, 128), i32),
            pltpu.SMEM((8, 128), i32),
            pltpu.SMEM((8, 128), i32),
            pltpu.VMEM((BINS * 32, 128), bf16),
            dma((2,)), dma((7,)), dma((2,)),
            dma((3,)), dma((3,)), dma((3,)), dma((3,)),
            dma((12,)), dma((12,)), dma((UNITS,)), dma((UNITS,)),
        ],
        compiler_params=pltpu.CompilerParams(collective_id=0, has_side_effects=True),
        name="dust_step",
    )(
        folded(dust_state), drift_speed, stop_ratio, folded(gas_rho), folded(gas_vel), folded(pressure),
        pair_list.T, outcome.T,
    )
    return unfolded(result)


def solution(mesh):
    return jax.shard_map(
        local,
        mesh=mesh,
        in_specs=(
            P(None, "bins", "tiles", None),
            P("bins"),
            P("bins"),
            P("tiles", None),
            P(None, "tiles", None),
            P("tiles", None),
            P(),
            P(None, "bins"),
        ),
        out_specs=P(None, "bins", "tiles", None),
        check_vma=False,
    )
```

```python
import functools

import jax
import jax.numpy as jnp
from jax import lax
from jax.experimental import pallas as pl
from jax.experimental.pallas import tpu as pltpu
from jax.sharding import PartitionSpec as P

MESH = pl.DeviceIdType.MESH
BINS = 112
LOCAL = 28
PAIRS = 6328
HALF = BINS // 2
UNITS = 7
GROUPS = 7
f32, bf16, i32 = jnp.float32, jnp.bfloat16, jnp.int32


def bin_at(group, member):
    if group < 6:
        tile = 2 * group + member // 8
        return tile // 3, (tile % 3) * 8 + member % 8
    return member // 4, 24 + member % 4


def group_member(index):
    shard = (index >= 28).astype(i32) + (index >= 56).astype(i32) + (index >= 84).astype(i32)
    own = index - 28 * shard
    tile = 3 * shard + (own >> 3)
    full = own < 24
    group = jnp.where(full, tile >> 1, 6)
    member = jnp.where(full, ((tile & 1) << 3) + (own & 7), 4 * shard + own - 24)
    return group, member


def slots_of(pairs):
    group_i, member_i = group_member(pairs[0:1, :])
    group_j, member_j = group_member(pairs[1:2, :])
    ahead = group_j - group_i
    ahead = jnp.where(ahead < 0, ahead + GROUPS, ahead)
    keep = ahead <= 3
    row = jnp.where(keep, group_i * 16 + member_i, group_j * 16 + member_j)
    slot = jnp.where(keep, ahead * 16 + member_j, (GROUPS - ahead) * 16 + member_i)
    return row, slot


def invert_pairs(pairs_ref, table_ref, core):
    total = jnp.zeros((HALF, 128), f32)
    for start in range(0, PAIRS, 256):
        width = min(256, PAIRS - start)
        row, slot = slots_of(pairs_ref[:, start : start + width])
        rows = lax.broadcasted_iota(i32, (HALF, width), 0)
        lanes = lax.broadcasted_iota(i32, (128, width), 0)
        number = start + 1 + lax.broadcasted_iota(i32, (1, width), 1)
        high = (number >> 6).astype(f32)
        low = (number & 63).astype(f32)
        value = jnp.where(lanes < 64, high, low)
        first = jnp.where(rows == row - HALF * core, 1.0, 0.0).astype(bf16)
        second = jnp.where((lanes & 63) == slot, value, 0.0).astype(bf16)
        total += lax.dot_general(first, second, (((1,), (1,)), ((), ())), preferred_element_type=f32)
    number = total * 64.0 + pltpu.roll(total, 64, 1)
    table_ref[...] = jnp.clip(number.astype(i32) - 1, 0, PAIRS - 1)


def turn_outcome(outcome_ref, turned_ref):
    for start in range(0, PAIRS, 128):
        width = min(128, PAIRS - start)
        turned_ref[start : start + width, 0:LOCAL] = outcome_ref[:, start : start + width].T


def gather_two(table, turned, held, two):
    for half in range(2):
        member = 2 * two + half
        for slot in range(member, 64):
            at = half * 64 + slot
            index = table[member, slot]
            held[at : at + 1, :] = turned[pl.ds(index, 1), :]


def place_two(value, rates, unit, two):
    lane = lax.broadcasted_iota(i32, (32, 128), 1)
    left = lane < 64
    member = lax.rem(unit, 2) * 8 + 2 * two
    value = jnp.where((lane & 63) < jnp.where(left, member, member + 1), 0.0, value)
    high = value.astype(bf16).astype(f32)
    low = pltpu.roll(value - high, 64, 1)
    start = pl.multiple_of(unit * 256 + two * 64, 64)
    rates[pl.ds(start, 32), :] = jnp.where(left, high, low).astype(bf16)
    rates[pl.ds(start + 32, 32), :] = jnp.where(left, low, high).astype(bf16)


def transported(own, before, after, speed):
    forward = jnp.maximum(speed, 0.0)
    backward = jnp.maximum(-speed, 0.0)

    def weights(a):
        square = a * a
        return (2.0 * a - 3.0 * square, 2.75 * square - 0.5 * a, -square, 0.125 * square)

    a = forward + backward
    row = lax.broadcasted_iota(i32, (8, 128), 0) & 3
    result = (1.0 - 1.5 * a + 1.125 * (a * a)) * own
    up, down = weights(forward), weights(backward)
    for m in (1, 2, 3):
        result += up[m - 1] * jnp.where(row >= m, pltpu.roll(own, m, 0), pltpu.roll(before, 4 + m, 0))
        result += down[m - 1] * jnp.where(row < 4 - m, pltpu.roll(own, 8 - m, 0), pltpu.roll(after, 4 - m, 0))
    return result + up[3] * before + down[3] * after


def step_kernel(
    dust_in, speed_in, stop_in, rho_in, vel_in, pres_in, pairs_in, outcome_in, out,
    own, before, after, pres_before, pres_after, dens, high, low, source,
    speed, stop, rho, vel, pres, pairs, outcome,
    turned, held, turns, table_v, table_a, table_b, rates,
    own_sem, in_sem, table_sem, up_send, up_recv, down_send, down_recv, ring_send, ring_recv, turn_send, turn_recv,
):
    tile, shard = lax.axis_index("tiles"), lax.axis_index("bins")
    tiles, shards = lax.axis_size("tiles"), lax.axis_size("bins")
    has_before, has_after = tile > 0, tile < tiles - 1
    core = lax.rem(tile, 2)
    nxt, prv = lax.rem(shard + 1, shards), lax.rem(shard + shards - 1, shards)

    barrier = pltpu.get_barrier_semaphore()
    pl.semaphore_signal(barrier, inc=1, device_id={"bins": nxt}, device_id_type=MESH)
    pl.semaphore_signal(barrier, inc=1, device_id={"bins": prv}, device_id_type=MESH)

    @pl.when(has_before)
    def _():
        pl.semaphore_signal(barrier, inc=1, device_id={"tiles": tile - 1}, device_id_type=MESH)

    @pl.when(has_after)
    def _():
        pl.semaphore_signal(barrier, inc=1, device_id={"tiles": tile + 1}, device_id_type=MESH)

    own_copies = [
        pltpu.make_async_copy(dust_in.at[0:1], own.at[0:1], own_sem.at[0]),
        pltpu.make_async_copy(dust_in.at[1:4], own.at[1:4], own_sem.at[1]),
    ]
    moves = ((pairs_in, pairs), (speed_in, speed), (outcome_in, outcome), (stop_in, stop), (rho_in, rho), (vel_in, vel), (pres_in, pres))
    pairs_copy, speed_copy, outcome_copy, *late_copies = [
        pltpu.make_async_copy(source_ref, target_ref, in_sem.at[i]) for i, (source_ref, target_ref) in enumerate(moves)
    ]
    pairs_copy.start()
    own_copies[0].start()
    speed_copy.start()
    outcome_copy.start()
    own_copies[1].start()
    for copy in late_copies:
        copy.start()

    pl.semaphore_wait(barrier, 2 + has_before.astype(i32) + has_after.astype(i32))

    def tile_copies(send, recv, target, there, pres_there):
        make = functools.partial(pltpu.make_async_remote_copy, device_id={"tiles": target}, device_id_type=MESH)
        return [
            make(dust_in.at[0:1], there.at[0:1], send.at[0], recv.at[0]),
            make(pres_in, pres_there, send.at[1], recv.at[1]),
            make(dust_in.at[1:4], there.at[1:4], send.at[2], recv.at[2]),
        ]

    ups = tile_copies(up_send, up_recv, tile + 1, before, pres_before)
    downs = tile_copies(down_send, down_recv, tile - 1, after, pres_after)

    for part in range(3):
        @pl.when(has_after)
        def _():
            ups[part].start()

        @pl.when(has_before)
        def _():
            downs[part].start()

    @pl.when(jnp.logical_not(has_before))
    def _():
        before[...] = jnp.zeros_like(before)
        pres_before[...] = jnp.zeros_like(pres_before)

    @pl.when(jnp.logical_not(has_after))
    def _():
        after[...] = jnp.zeros_like(after)
        pres_after[...] = jnp.zeros_like(pres_after)

    def arrived(part):
        @pl.when(has_before)
        def _():
            ups[part].wait_recv()

        @pl.when(has_after)
        def _():
            downs[part].wait_recv()

    pairs_copy.wait()
    invert_pairs(pairs, table_v, core)

    tables = (table_a, table_b)

    def table_copy(unit):
        return pltpu.make_async_copy(table_v.at[8 * unit : 8 * unit + 8, :], tables[unit % 2], table_sem.at[unit % 2])

    table_copy(0).start()
    table_copy(1).start()
    outcome_copy.wait()
    turn_outcome(outcome, turned)

    own_copies[0].wait()
    speed_copy.wait()
    arrived(0)
    here = shard * 224
    for k in range(LOCAL):
        moved = transported(own[0, k], before[0, k], after[0, k], jnp.full((8, 128), speed[k], f32))
        out[0, k] = moved
        dens[pl.ds(here + k, 8, stride=LOCAL), :] = moved

    def ring_copy(block, chunk, target, slot):
        piece = dens.at[pl.ds(pl.multiple_of(block * 224 + chunk * 56, 8), 56), :]
        return pltpu.make_async_remote_copy(
            piece, piece, ring_send.at[slot], ring_recv.at[slot],
            device_id={"bins": target}, device_id_type=MESH,
        )

    two_back = lax.rem(shard + 2, shards)
    forward, backward, relayed = (0, 1, 2, 3), (2, 3, 0, 1), (0, 2, 1, 3)
    sends = []
    for i in range(4):
        sends.append(ring_copy(shard, forward[i], nxt, forward[i]))
        sends.append(ring_copy(shard, backward[i], prv, 4 + backward[i]))
    for copy in sends:
        copy.start()
    from_prv = [ring_copy(prv, c, nxt, c) for c in range(4)]
    from_nxt = [ring_copy(nxt, c, prv, 4 + c) for c in range(4)]
    relays = [ring_copy(prv, c, nxt, 8 + c) if c < 2 else ring_copy(nxt, c, prv, 8 + c) for c in range(4)]
    far = [ring_copy(two_back, c, nxt if c < 2 else prv, 8 + c) for c in range(4)]

    first_unit = core * UNITS
    other_unit = UNITS - first_unit

    def turn_copy(unit):
        piece = turns.at[pl.ds((first_unit + unit) * 4, 4)]
        return pltpu.make_async_remote_copy(
            piece, piece, turn_send.at[unit], turn_recv.at[unit],
            device_id={"tiles": tile + 1 - 2 * core}, device_id_type=MESH,
        )

    def arriving(unit):
        piece = turns.at[pl.ds((other_unit + unit) * 4, 4)]
        return pltpu.make_async_remote_copy(
            piece, piece, turn_send.at[unit], turn_recv.at[unit],
            device_id={"tiles": tile + 1 - 2 * core}, device_id_type=MESH,
        )

    def finish(unit, two):
        value = held[(unit % 2) * 4 + two].T[0:32, :]
        turns[(first_unit + unit) * 4 + two] = value
        place_two(value, rates, first_unit + unit, two)

    def sort_unit(unit):
        table_copy(unit).wait()
        for two in range(4):
            gather_two(tables[unit % 2], turned, held.at[(unit % 2) * 4 + two], two)
            if two > 0:
                finish(unit, two - 1)
            elif unit > 0:
                finish(unit - 1, 3)
        if unit > 0:
            turn_copy(unit - 1).start()
        if unit + 2 < UNITS:
            table_copy(unit + 2).start()

    def relay(c):
        (from_prv if c < 2 else from_nxt)[c].wait_recv()
        relays[c].start()

    for unit in range(6):
        sort_unit(unit)
    relay(0)
    relay(2)
    sort_unit(6)
    finish(6, 3)

    own_copies[1].wait()
    arrived(1)
    arrived(2)
    turn_copy(6).start()

    def momenta(k, carry):
        rate = jnp.full((8, 128), speed[k], f32)
        for d in range(1, 4):
            out[d, k] = transported(own[d, k], before[d, k], after[d, k], rate)
        return carry

    lax.fori_loop(0, LOCAL, momenta, 0)
    relay(1)
    relay(3)

    for unit in range(UNITS):
        arriving(unit).wait_recv()

    def place_unit(unit, carry):
        for two in range(4):
            place_two(turns[(other_unit + unit) * 4 + two], rates, other_unit + unit, two)
        return carry

    lax.fori_loop(0, UNITS, place_unit, 0)

    for c in range(2):
        from_prv[2 + c].wait_recv()
        from_nxt[c].wait_recv()

    for c in relayed:
        far[c].wait_recv()
        for m in (2 * c, 2 * c + 1):
            for group in range(GROUPS):
                if group < 6:
                    starts = [bin_at(group, 0), bin_at(group, 8)]
                    pieces = [dens[b * 224 + m * 28 + w : b * 224 + m * 28 + w + 8, :] for b, w in starts]
                else:
                    pieces = [dens[b * 224 + m * 28 + 24 : b * 224 + m * 28 + 28, :] for b in range(4)]
                value = jnp.concatenate(pieces, 0)
                top = value.astype(bf16)
                rest = (value - top.astype(f32)).astype(bf16)
                for at in (group, group + GROUPS):
                    if at < 10:
                        high[at * 16 : at * 16 + 16, m * 128 : m * 128 + 128] = top
                        low[at * 16 : at * 16 + 16, m * 128 : m * 128 + 128] = rest
        total = jnp.zeros((32, 256), f32)
        for group in range(GROUPS):
            top = high[group * 16 : group * 16 + 64, c * 256 : c * 256 + 256]
            rest = low[group * 16 : group * 16 + 64, c * 256 : c * 256 + 256]
            weights = jnp.concatenate([top, top, rest, rest], 0)
            block = rates[group * 512 : group * 512 + 512, :]
            product = jnp.dot(jnp.concatenate([block, block], 1), weights, preferred_element_type=f32)
            for member in range(16):
                b, w = bin_at(group, member)
                start = b * 224 + w + c * 56
                line = jnp.concatenate([dens[start : start + 1, :], dens[start + 28 : start + 29, :]], 1)
                total += product[member * 32 : member * 32 + 32, :] * line
        for half in range(2):
            for k in range(4):
                source[pl.ds(k * 64 + 2 * c + half, 8, stride=8), :] = total[k * 8 : k * 8 + 8, half * 128 : half * 128 + 128]

    for copy in late_copies:
        copy.wait()
    row = lax.broadcasted_iota(i32, (8, 128), 0) & 3
    here_p = pres[...]
    above = jnp.where(row < 3, pltpu.roll(here_p, 7, 0), pltpu.roll(pres_after[...], 3, 0))
    below = jnp.where(row >= 1, pltpu.roll(here_p, 1, 0), pltpu.roll(pres_before[...], 5, 0))
    gradient = (above - below) / (2.0 * rho[...])
    gas = [vel[d] for d in range(3)]
    target = [gas[0] - gradient, gas[1], gas[2]]

    for k in range(LOCAL):
        half = 0.5 * source[k * 8 : k * 8 + 8, :]
        density = out[0, k] + half
        s = jnp.full((8, 128), stop[k], f32)
        share = 1.0 / (1.0 + s)
        pull = s * density
        out[0, k] = density
        for d in range(3):
            grown = out[d + 1, k] + half * gas[d]
            out[d + 1, k] = (grown + pull * target[d]) * share

    for copy in (*sends, *relays, *[turn_copy(unit) for unit in range(UNITS)]):
        copy.wait_send()
    for part in range(3):
        @pl.when(has_after)
        def _():
            ups[part].wait_send()

        @pl.when(has_before)
        def _():
            downs[part].wait_send()


def folded(value):
    lead = value.shape[:-2]
    value = value.reshape(*lead, 4, 2, 128)
    return jnp.swapaxes(value, -3, -2).reshape(*lead, 8, 128)


def unfolded(value):
    lead = value.shape[:-2]
    value = value.reshape(*lead, 2, 4, 128)
    return jnp.swapaxes(value, -3, -2).reshape(*lead, 4, 256)


def local(dust_state, drift_speed, stop_ratio, gas_rho, gas_vel, pressure, pair_list, outcome):
    halo = pltpu.VMEM((4, LOCAL, 8, 128), f32)
    cell = pltpu.VMEM((8, 128), f32)
    dma = pltpu.SemaphoreType.DMA
    result = pl.pallas_call(
        step_kernel,
        out_shape=pltpu.VMEM((4, LOCAL, 8, 128), f32),
        in_specs=[pl.BlockSpec(memory_space=pl.ANY)] * 8,
        out_specs=pl.BlockSpec(memory_space=pltpu.VMEM),
        scratch_shapes=[
            halo, halo, halo, cell, cell,
            pltpu.VMEM((4 * 224, 128), f32),
            pltpu.VMEM((160, 1024), bf16),
            pltpu.VMEM((160, 1024), bf16),
            pltpu.VMEM((256, 128), f32),
            pltpu.SMEM((LOCAL,), f32),
            pltpu.SMEM((LOCAL,), f32),
            cell,
            pltpu.VMEM((3, 8, 128), f32),
            cell,
            pltpu.VMEM((2, PAIRS), i32),
            pltpu.VMEM((LOCAL, PAIRS), f32),
            pltpu.VMEM((PAIRS, 128), f32),
            pltpu.VMEM((8, 128, 128), f32),
            pltpu.VMEM((2 * UNITS * 4, 32, 128), f32),
            pltpu.VMEM((HALF, 128), i32),
            pltpu.SMEM((8, 128), i32),
            pltpu.SMEM((8, 128), i32),
            pltpu.VMEM((BINS * 32, 128), bf16),
            dma((2,)), dma((7,)), dma((2,)),
            dma((3,)), dma((3,)), dma((3,)), dma((3,)),
            dma((12,)), dma((12,)), dma((UNITS,)), dma((UNITS,)),
        ],
        compiler_params=pltpu.CompilerParams(collective_id=0, has_side_effects=True),
        name="dust_step",
    )(
        folded(dust_state), drift_speed, stop_ratio, folded(gas_rho), folded(gas_vel), folded(pressure),
        pair_list.T, outcome.T,
    )
    return unfolded(result)


def solution(mesh):
    return jax.shard_map(
        local,
        mesh=mesh,
        in_specs=(
            P(None, "bins", "tiles", None),
            P("bins"),
            P("bins"),
            P("tiles", None),
            P(None, "tiles", None),
            P("tiles", None),
            P(),
            P(None, "bins"),
        ),
        out_specs=P(None, "bins", "tiles", None),
        check_vma=False,
    )
```

```python
import functools

import jax
import jax.numpy as jnp
from jax import lax
from jax.experimental import pallas as pl
from jax.experimental.pallas import tpu as pltpu
from jax.sharding import PartitionSpec as P

MESH = pl.DeviceIdType.MESH
BINS = 112
LOCAL = 28
PAIRS = 6328
HALF = BINS // 2
UNITS = 7
GROUPS = 7
f32, bf16, i32 = jnp.float32, jnp.bfloat16, jnp.int32


def bin_at(group, member):
    tile, low = 2 * group + member // 8, member % 8
    if tile < 9:
        return tile // 3, (tile % 3) * 8 + low
    if tile == 9:
        return low // 4, 24 + low % 4
    if tile < 13:
        return 3, (tile - 10) * 8 + low
    return 2 + low // 4, 24 + low % 4


def group_member(index, shard):
    owner = (index >= 28).astype(i32) + (index >= 56).astype(i32) + (index >= 84).astype(i32)
    own = index - 28 * owner
    ahead = (owner - shard) & 3
    block = jnp.where(ahead == 2, 3, jnp.where(ahead == 3, 2, ahead))
    full = jnp.where(block == 3, 10, 3 * block) + (own >> 3)
    left = jnp.where(block < 2, 9, 13)
    is_full = own < 24
    tile = jnp.where(is_full, full, left)
    low = jnp.where(is_full, own & 7, ((block & 1) << 2) + own - 24)
    return tile >> 1, ((tile & 1) << 3) + low


def slots_of(pairs, shard):
    group_i, member_i = group_member(pairs[0:1, :], shard)
    group_j, member_j = group_member(pairs[1:2, :], shard)
    ahead = group_j - group_i
    ahead = jnp.where(ahead < 0, ahead + GROUPS, ahead)
    keep = (ahead <= 3) & ((ahead > 0) | (member_i <= member_j))
    ahead = jnp.where((ahead == 0) & ~keep, GROUPS, ahead)
    row = jnp.where(keep, group_i * 16 + member_i, group_j * 16 + member_j)
    slot = jnp.where(keep, ahead * 16 + member_j, (GROUPS - ahead) * 16 + member_i)
    return row, slot


def invert_pairs(pairs_ref, table_ref, core, shard):
    total = jnp.zeros((HALF, 128), f32)
    for start in range(0, PAIRS, 256):
        width = min(256, PAIRS - start)
        row, slot = slots_of(pairs_ref[:, start : start + width], shard)
        rows = lax.broadcasted_iota(i32, (HALF, width), 0)
        lanes = lax.broadcasted_iota(i32, (128, width), 0)
        number = start + 1 + lax.broadcasted_iota(i32, (1, width), 1)
        high = (number >> 6).astype(f32)
        low = (number & 63).astype(f32)
        value = jnp.where(lanes < 64, high, low)
        first = jnp.where(rows == row - HALF * core, 1.0, 0.0).astype(bf16)
        second = jnp.where((lanes & 63) == slot, value, 0.0).astype(bf16)
        total += lax.dot_general(first, second, (((1,), (1,)), ((), ())), preferred_element_type=f32)
    number = total * 64.0 + pltpu.roll(total, 64, 1)
    table_ref[...] = jnp.clip(number.astype(i32) - 1, 0, PAIRS - 1)


def turn_outcome(outcome_ref, turned_ref):
    for start in range(0, PAIRS, 128):
        width = min(128, PAIRS - start)
        turned_ref[start : start + width, 0:LOCAL] = outcome_ref[:, start : start + width].T


def gather_two(table, turned, held, two):
    for half in range(2):
        member = 2 * two + half
        for slot in range(member, 64):
            at = half * 64 + slot
            index = table[member, slot]
            held[at : at + 1, :] = turned[pl.ds(index, 1), :]


def place_two(value, rates, unit, two):
    lane = lax.broadcasted_iota(i32, (32, 128), 1)
    left = lane < 64
    member = lax.rem(unit, 2) * 8 + 2 * two
    value = jnp.where((lane & 63) < jnp.where(left, member, member + 1), 0.0, value)
    high = value.astype(bf16).astype(f32)
    low = pltpu.roll(value - high, 64, 1)
    start = pl.multiple_of(unit * 256 + two * 64, 64)
    rates[pl.ds(start, 32), :] = jnp.where(left, high, low).astype(bf16)
    rates[pl.ds(start + 32, 32), :] = jnp.where(left, low, high).astype(bf16)


def transported(own, before, after, speed):
    forward = jnp.maximum(speed, 0.0)
    backward = jnp.maximum(-speed, 0.0)

    def weights(a):
        square = a * a
        return (2.0 * a - 3.0 * square, 2.75 * square - 0.5 * a, -square, 0.125 * square)

    a = forward + backward
    row = lax.broadcasted_iota(i32, (8, 128), 0) & 3
    result = (1.0 - 1.5 * a + 1.125 * (a * a)) * own
    up, down = weights(forward), weights(backward)
    for m in (1, 2, 3):
        result += up[m - 1] * jnp.where(row >= m, pltpu.roll(own, m, 0), pltpu.roll(before, 4 + m, 0))
        result += down[m - 1] * jnp.where(row < 4 - m, pltpu.roll(own, 8 - m, 0), pltpu.roll(after, 4 - m, 0))
    return result + up[3] * before + down[3] * after


def step_kernel(
    dust_in, speed_in, stop_in, rho_in, vel_in, pres_in, pairs_in, outcome_in, out,
    own, before, after, pres_before, pres_after, dens, high, low, partial, source,
    speed, stop, rho, vel, pres, pairs, outcome,
    turned, held, turns, table_v, table_a, table_b, rates,
    own_sem, in_sem, table_sem, up_send, up_recv, down_send, down_recv, ring_send, ring_recv, turn_send, turn_recv,
):
    tile, shard = lax.axis_index("tiles"), lax.axis_index("bins")
    tiles, shards = lax.axis_size("tiles"), lax.axis_size("bins")
    has_before, has_after = tile > 0, tile < tiles - 1
    core = lax.rem(tile, 2)
    nxt, prv = lax.rem(shard + 1, shards), lax.rem(shard + shards - 1, shards)

    barrier = pltpu.get_barrier_semaphore()
    pl.semaphore_signal(barrier, inc=1, device_id={"bins": nxt}, device_id_type=MESH)
    pl.semaphore_signal(barrier, inc=1, device_id={"bins": prv}, device_id_type=MESH)

    @pl.when(has_before)
    def _():
        pl.semaphore_signal(barrier, inc=1, device_id={"tiles": tile - 1}, device_id_type=MESH)

    @pl.when(has_after)
    def _():
        pl.semaphore_signal(barrier, inc=1, device_id={"tiles": tile + 1}, device_id_type=MESH)

    own_copies = [
        pltpu.make_async_copy(dust_in.at[0:1], own.at[0:1], own_sem.at[0]),
        pltpu.make_async_copy(dust_in.at[1:4], own.at[1:4], own_sem.at[1]),
    ]
    moves = ((pairs_in, pairs), (speed_in, speed), (outcome_in, outcome), (stop_in, stop), (rho_in, rho), (vel_in, vel), (pres_in, pres))
    pairs_copy, speed_copy, outcome_copy, *late_copies = [
        pltpu.make_async_copy(source_ref, target_ref, in_sem.at[i]) for i, (source_ref, target_ref) in enumerate(moves)
    ]
    pairs_copy.start()
    own_copies[0].start()
    speed_copy.start()
    outcome_copy.start()
    own_copies[1].start()
    for copy in late_copies:
        copy.start()

    pl.semaphore_wait(barrier, 2 + has_before.astype(i32) + has_after.astype(i32))

    def tile_copies(send, recv, target, there, pres_there):
        make = functools.partial(pltpu.make_async_remote_copy, device_id={"tiles": target}, device_id_type=MESH)
        return [
            make(dust_in.at[0:1], there.at[0:1], send.at[0], recv.at[0]),
            make(pres_in, pres_there, send.at[1], recv.at[1]),
            make(dust_in.at[1:4], there.at[1:4], send.at[2], recv.at[2]),
        ]

    ups = tile_copies(up_send, up_recv, tile + 1, before, pres_before)
    downs = tile_copies(down_send, down_recv, tile - 1, after, pres_after)

    for part in range(3):
        @pl.when(has_after)
        def _():
            ups[part].start()

        @pl.when(has_before)
        def _():
            downs[part].start()

    @pl.when(jnp.logical_not(has_before))
    def _():
        before[...] = jnp.zeros_like(before)
        pres_before[...] = jnp.zeros_like(pres_before)

    @pl.when(jnp.logical_not(has_after))
    def _():
        after[...] = jnp.zeros_like(after)
        pres_after[...] = jnp.zeros_like(pres_after)

    def arrived(part):
        @pl.when(has_before)
        def _():
            ups[part].wait_recv()

        @pl.when(has_after)
        def _():
            downs[part].wait_recv()

    pairs_copy.wait()
    invert_pairs(pairs, table_v, core, shard)

    tables = (table_a, table_b)

    def table_copy(unit):
        return pltpu.make_async_copy(table_v.at[8 * unit : 8 * unit + 8, :], tables[unit % 2], table_sem.at[unit % 2])

    table_copy(0).start()
    table_copy(1).start()
    outcome_copy.wait()
    turn_outcome(outcome, turned)

    own_copies[0].wait()
    speed_copy.wait()
    arrived(0)
    for k in range(LOCAL):
        moved = transported(own[0, k], before[0, k], after[0, k], jnp.full((8, 128), speed[k], f32))
        out[0, k] = moved
        dens[pl.ds(k, 8, stride=LOCAL), :] = moved

    def ring_copy(block, there, chunk, target, slot):
        make = lambda at: dens.at[at * 224 + chunk * 56 : at * 224 + chunk * 56 + 56, :]
        return pltpu.make_async_remote_copy(
            make(block), make(there), ring_send.at[slot], ring_recv.at[slot],
            device_id={"bins": target}, device_id_type=MESH,
        )

    forward, backward, relayed = (0, 1, 2, 3), (2, 3, 0, 1), (0, 2, 1, 3)
    to_nxt = [ring_copy(0, 2, c, nxt, c) for c in range(4)]
    to_prv = [ring_copy(0, 1, c, prv, 4 + c) for c in range(4)]
    relays = [ring_copy(2, 3, c, nxt, 8 + c) if c < 2 else ring_copy(1, 3, c, prv, 8 + c) for c in range(4)]
    sends = []
    for i in range(4):
        sends += [to_nxt[forward[i]], to_prv[backward[i]]]
    for copy in sends:
        copy.start()

    first_unit = core * UNITS
    other_unit = UNITS - first_unit

    def turn_copy(unit):
        piece = turns.at[pl.ds((first_unit + unit) * 4, 4)]
        return pltpu.make_async_remote_copy(
            piece, piece, turn_send.at[unit], turn_recv.at[unit],
            device_id={"tiles": tile + 1 - 2 * core}, device_id_type=MESH,
        )

    def arriving(unit):
        piece = turns.at[pl.ds((other_unit + unit) * 4, 4)]
        return pltpu.make_async_remote_copy(
            piece, piece, turn_send.at[unit], turn_recv.at[unit],
            device_id={"tiles": tile + 1 - 2 * core}, device_id_type=MESH,
        )

    def finish(unit, two):
        value = held[(unit % 2) * 4 + two].T[0:32, :]
        turns[(first_unit + unit) * 4 + two] = value
        place_two(value, rates, first_unit + unit, two)

    def sort_unit(unit):
        table_copy(unit).wait()
        for two in range(4):
            gather_two(tables[unit % 2], turned, held.at[(unit % 2) * 4 + two], two)
            if two > 0:
                finish(unit, two - 1)
            elif unit > 0:
                finish(unit - 1, 3)
        if unit > 0:
            turn_copy(unit - 1).start()
        if unit + 2 < UNITS:
            table_copy(unit + 2).start()

    def relay(c):
        (to_nxt if c < 2 else to_prv)[c].wait_recv()
        relays[c].start()

    for unit in range(6):
        sort_unit(unit)
    relay(0)
    relay(2)
    sort_unit(6)
    finish(6, 3)

    own_copies[1].wait()
    arrived(1)
    arrived(2)
    turn_copy(6).start()

    def momenta(k, carry):
        rate = jnp.full((8, 128), speed[k], f32)
        for d in range(1, 4):
            out[d, k] = transported(own[d, k], before[d, k], after[d, k], rate)
        return carry

    lax.fori_loop(0, LOCAL, momenta, 0)
    relay(1)
    relay(3)

    for unit in range(UNITS):
        arriving(unit).wait_recv()

    def place_unit(unit, carry):
        for two in range(4):
            place_two(turns[(other_unit + unit) * 4 + two], rates, other_unit + unit, two)
        return carry

    lax.fori_loop(0, UNITS, place_unit, 0)

    for c in range(2):
        to_nxt[2 + c].wait_recv()
        to_prv[c].wait_recv()

    def split(c, groups):
        for m in (2 * c, 2 * c + 1):
            for group in groups:
                pieces, member = [], 0
                while member < 16:
                    b, w = bin_at(group, member)
                    size = 8 if w < 24 else 4
                    start = b * 224 + m * 28 + w
                    pieces.append(dens[start : start + size, :])
                    member += size
                value = jnp.concatenate(pieces, 0)
                top = value.astype(bf16)
                rest = (value - top.astype(f32)).astype(bf16)
                for at in (group, group + GROUPS):
                    if at < 10:
                        high[at * 16 : at * 16 + 16, m * 128 : m * 128 + 128] = top
                        low[at * 16 : at * 16 + 16, m * 128 : m * 128 + 128] = rest

    def multiply(c, groups, total):
        for group in groups:
            top = high[group * 16 : group * 16 + 64, c * 256 : c * 256 + 256]
            rest = low[group * 16 : group * 16 + 64, c * 256 : c * 256 + 256]
            weights = jnp.concatenate([top, top, rest, rest], 0)
            block = rates[group * 512 : group * 512 + 512, :]
            product = jnp.dot(jnp.concatenate([block, block], 1), weights, preferred_element_type=f32)
            for member in range(16):
                b, w = bin_at(group, member)
                start = b * 224 + w + c * 56
                line = jnp.concatenate([dens[start : start + 1, :], dens[start + 28 : start + 29, :]], 1)
                total += product[member * 32 : member * 32 + 32, :] * line
        return total

    for c in relayed:
        split(c, range(5))
        partial[c] = multiply(c, range(2), jnp.zeros((32, 256), f32))

    for c in relayed:
        relays[c].wait_recv()
        split(c, range(5, GROUPS))
        total = multiply(c, range(2, GROUPS), partial[c])
        for half in range(2):
            for k in range(4):
                source[pl.ds(k * 64 + 2 * c + half, 8, stride=8), :] = total[k * 8 : k * 8 + 8, half * 128 : half * 128 + 128]

    for copy in late_copies:
        copy.wait()
    row = lax.broadcasted_iota(i32, (8, 128), 0) & 3
    here_p = pres[...]
    above = jnp.where(row < 3, pltpu.roll(here_p, 7, 0), pltpu.roll(pres_after[...], 3, 0))
    below = jnp.where(row >= 1, pltpu.roll(here_p, 1, 0), pltpu.roll(pres_before[...], 5, 0))
    gradient = (above - below) / (2.0 * rho[...])
    gas = [vel[d] for d in range(3)]
    target = [gas[0] - gradient, gas[1], gas[2]]

    for k in range(LOCAL):
        half = 0.5 * source[k * 8 : k * 8 + 8, :]
        density = out[0, k] + half
        s = jnp.full((8, 128), stop[k], f32)
        share = 1.0 / (1.0 + s)
        pull = s * density
        out[0, k] = density
        for d in range(3):
            grown = out[d + 1, k] + half * gas[d]
            out[d + 1, k] = (grown + pull * target[d]) * share

    for copy in (*sends, *relays, *[turn_copy(unit) for unit in range(UNITS)]):
        copy.wait_send()
    for part in range(3):
        @pl.when(has_after)
        def _():
            ups[part].wait_send()

        @pl.when(has_before)
        def _():
            downs[part].wait_send()


def folded(value):
    lead = value.shape[:-2]
    value = value.reshape(*lead, 4, 2, 128)
    return jnp.swapaxes(value, -3, -2).reshape(*lead, 8, 128)


def unfolded(value):
    lead = value.shape[:-2]
    value = value.reshape(*lead, 2, 4, 128)
    return jnp.swapaxes(value, -3, -2).reshape(*lead, 4, 256)


def local(dust_state, drift_speed, stop_ratio, gas_rho, gas_vel, pressure, pair_list, outcome):
    halo = pltpu.VMEM((4, LOCAL, 8, 128), f32)
    cell = pltpu.VMEM((8, 128), f32)
    dma = pltpu.SemaphoreType.DMA
    result = pl.pallas_call(
        step_kernel,
        out_shape=pltpu.VMEM((4, LOCAL, 8, 128), f32),
        in_specs=[pl.BlockSpec(memory_space=pl.ANY)] * 8,
        out_specs=pl.BlockSpec(memory_space=pltpu.VMEM),
        scratch_shapes=[
            halo, halo, halo, cell, cell,
            pltpu.VMEM((4 * 224, 128), f32),
            pltpu.VMEM((160, 1024), bf16),
            pltpu.VMEM((160, 1024), bf16),
            pltpu.VMEM((4, 32, 256), f32),
            pltpu.VMEM((256, 128), f32),
            pltpu.SMEM((LOCAL,), f32),
            pltpu.SMEM((LOCAL,), f32),
            cell,
            pltpu.VMEM((3, 8, 128), f32),
            cell,
            pltpu.VMEM((2, PAIRS), i32),
            pltpu.VMEM((LOCAL, PAIRS), f32),
            pltpu.VMEM((PAIRS, 128), f32),
            pltpu.VMEM((8, 128, 128), f32),
            pltpu.VMEM((2 * UNITS * 4, 32, 128), f32),
            pltpu.VMEM((HALF, 128), i32),
            pltpu.SMEM((8, 128), i32),
            pltpu.SMEM((8, 128), i32),
            pltpu.VMEM((BINS * 32, 128), bf16),
            dma((2,)), dma((7,)), dma((2,)),
            dma((3,)), dma((3,)), dma((3,)), dma((3,)),
            dma((12,)), dma((12,)), dma((UNITS,)), dma((UNITS,)),
        ],
        compiler_params=pltpu.CompilerParams(collective_id=0, has_side_effects=True),
        name="dust_step",
    )(
        folded(dust_state), drift_speed, stop_ratio, folded(gas_rho), folded(gas_vel), folded(pressure),
        pair_list.T, outcome.T,
    )
    return unfolded(result)


def solution(mesh):
    return jax.shard_map(
        local,
        mesh=mesh,
        in_specs=(
            P(None, "bins", "tiles", None),
            P("bins"),
            P("bins"),
            P("tiles", None),
            P(None, "tiles", None),
            P("tiles", None),
            P(),
            P(None, "bins"),
        ),
        out_specs=P(None, "bins", "tiles", None),
        check_vma=False,
    )
```

```python
import functools

import jax
import jax.numpy as jnp
from jax import lax
from jax.experimental import pallas as pl
from jax.experimental.pallas import tpu as pltpu
from jax.sharding import PartitionSpec as P

MESH = pl.DeviceIdType.MESH
BINS = 112
LOCAL = 28
PAIRS = 6328
HALF = BINS // 2
UNITS = 7
GROUPS = 7
f32, bf16, i32 = jnp.float32, jnp.bfloat16, jnp.int32


def bin_at(group, member):
    tile, low = 2 * group + member // 8, member % 8
    if tile < 9:
        return tile // 3, (tile % 3) * 8 + low
    if tile == 9:
        return low // 4, 24 + low % 4
    if tile < 13:
        return 3, (tile - 10) * 8 + low
    return 2 + low // 4, 24 + low % 4


def group_member(index, shard):
    owner = (index >= 28).astype(i32) + (index >= 56).astype(i32) + (index >= 84).astype(i32)
    own = index - 28 * owner
    ahead = (owner - shard) & 3
    block = jnp.where(ahead == 2, 3, jnp.where(ahead == 3, 2, ahead))
    full = jnp.where(block == 3, 10, 3 * block) + (own >> 3)
    left = jnp.where(block < 2, 9, 13)
    is_full = own < 24
    tile = jnp.where(is_full, full, left)
    low = jnp.where(is_full, own & 7, ((block & 1) << 2) + own - 24)
    return tile >> 1, ((tile & 1) << 3) + low


def slots_of(pairs, shard):
    group_i, member_i = group_member(pairs[0:1, :], shard)
    group_j, member_j = group_member(pairs[1:2, :], shard)
    ahead = group_j - group_i
    ahead = jnp.where(ahead < 0, ahead + GROUPS, ahead)
    keep = (ahead <= 3) & ((ahead > 0) | (member_i <= member_j))
    ahead = jnp.where((ahead == 0) & ~keep, GROUPS, ahead)
    row = jnp.where(keep, group_i * 16 + member_i, group_j * 16 + member_j)
    slot = jnp.where(keep, ahead * 16 + member_j, (GROUPS - ahead) * 16 + member_i)
    return row, slot


def invert_pairs(pairs_ref, table_ref, core, shard):
    total = jnp.zeros((HALF, 128), f32)
    for start in range(0, PAIRS, 256):
        width = min(256, PAIRS - start)
        row, slot = slots_of(pairs_ref[:, start : start + width], shard)
        rows = lax.broadcasted_iota(i32, (HALF, width), 0)
        lanes = lax.broadcasted_iota(i32, (128, width), 0)
        number = start + 1 + lax.broadcasted_iota(i32, (1, width), 1)
        high = (number >> 6).astype(f32)
        low = (number & 63).astype(f32)
        value = jnp.where(lanes < 64, high, low)
        first = jnp.where(rows == row - HALF * core, 1.0, 0.0).astype(bf16)
        second = jnp.where((lanes & 63) == slot, value, 0.0).astype(bf16)
        total += lax.dot_general(first, second, (((1,), (1,)), ((), ())), preferred_element_type=f32)
    number = total * 64.0 + pltpu.roll(total, 64, 1)
    table_ref[...] = jnp.clip(number.astype(i32) - 1, 0, PAIRS - 1)


def turn_outcome(outcome_ref, turned_ref):
    for start in range(0, PAIRS, 128):
        width = min(128, PAIRS - start)
        turned_ref[start : start + width, 0:LOCAL] = outcome_ref[:, start : start + width].T


def gather_two(table, turned, held, two):
    for half in range(2):
        member = 2 * two + half
        for slot in range(member, 64):
            at = half * 64 + slot
            index = table[member, slot]
            held[at : at + 1, :] = turned[pl.ds(index, 1), :]


def place_two(value, rates, unit, two):
    lane = lax.broadcasted_iota(i32, (32, 128), 1)
    left = lane < 64
    member = lax.rem(unit, 2) * 8 + 2 * two
    value = jnp.where((lane & 63) < jnp.where(left, member, member + 1), 0.0, value)
    high = value.astype(bf16).astype(f32)
    low = pltpu.roll(value - high, 64, 1)
    start = pl.multiple_of(unit * 256 + two * 64, 64)
    rates[pl.ds(start, 32), :] = jnp.where(left, high, low).astype(bf16)
    rates[pl.ds(start + 32, 32), :] = jnp.where(left, low, high).astype(bf16)


def transported(own, before, after, speed):
    forward = jnp.maximum(speed, 0.0)
    backward = jnp.maximum(-speed, 0.0)

    def weights(a):
        square = a * a
        return (2.0 * a - 3.0 * square, 2.75 * square - 0.5 * a, -square, 0.125 * square)

    a = forward + backward
    row = lax.broadcasted_iota(i32, (8, 128), 0) & 3
    result = (1.0 - 1.5 * a + 1.125 * (a * a)) * own
    up, down = weights(forward), weights(backward)
    for m in (1, 2, 3):
        result += up[m - 1] * jnp.where(row >= m, pltpu.roll(own, m, 0), pltpu.roll(before, 4 + m, 0))
        result += down[m - 1] * jnp.where(row < 4 - m, pltpu.roll(own, 8 - m, 0), pltpu.roll(after, 4 - m, 0))
    return result + up[3] * before + down[3] * after


def step_kernel(
    dust_in, speed_in, stop_in, rho_in, vel_in, pres_in, pairs_in, outcome_in, out,
    own, before, after, pres_before, pres_after, dens, high, low, partial, source,
    speed, stop, rho, vel, pres, pairs, outcome,
    turned, held, turns, table_v, table_a, table_b, rates,
    own_sem, in_sem, table_sem, up_send, up_recv, down_send, down_recv, ring_send, ring_recv, turn_send, turn_recv,
):
    tile, shard = lax.axis_index("tiles"), lax.axis_index("bins")
    tiles, shards = lax.axis_size("tiles"), lax.axis_size("bins")
    has_before, has_after = tile > 0, tile < tiles - 1
    core = lax.rem(tile, 2)
    nxt, prv = lax.rem(shard + 1, shards), lax.rem(shard + shards - 1, shards)

    barrier = pltpu.get_barrier_semaphore()
    pl.semaphore_signal(barrier, inc=1, device_id={"bins": nxt}, device_id_type=MESH)
    pl.semaphore_signal(barrier, inc=1, device_id={"bins": prv}, device_id_type=MESH)

    @pl.when(has_before)
    def _():
        pl.semaphore_signal(barrier, inc=1, device_id={"tiles": tile - 1}, device_id_type=MESH)

    @pl.when(has_after)
    def _():
        pl.semaphore_signal(barrier, inc=1, device_id={"tiles": tile + 1}, device_id_type=MESH)

    own_copies = [
        pltpu.make_async_copy(dust_in.at[0:1], own.at[0:1], own_sem.at[0]),
        pltpu.make_async_copy(dust_in.at[1:4], own.at[1:4], own_sem.at[1]),
    ]
    moves = ((pairs_in, pairs), (speed_in, speed), (outcome_in, outcome), (stop_in, stop), (rho_in, rho), (vel_in, vel), (pres_in, pres))
    pairs_copy, speed_copy, outcome_copy, *late_copies = [
        pltpu.make_async_copy(source_ref, target_ref, in_sem.at[i]) for i, (source_ref, target_ref) in enumerate(moves)
    ]
    pairs_copy.start()
    own_copies[0].start()
    speed_copy.start()
    outcome_copy.start()
    own_copies[1].start()
    for copy in late_copies:
        copy.start()

    pl.semaphore_wait(barrier, 2 + has_before.astype(i32) + has_after.astype(i32))

    def tile_copies(send, recv, target, there, pres_there):
        make = functools.partial(pltpu.make_async_remote_copy, device_id={"tiles": target}, device_id_type=MESH)
        return [
            make(dust_in.at[0:1], there.at[0:1], send.at[0], recv.at[0]),
            make(pres_in, pres_there, send.at[1], recv.at[1]),
            make(dust_in.at[1:4], there.at[1:4], send.at[2], recv.at[2]),
        ]

    ups = tile_copies(up_send, up_recv, tile + 1, before, pres_before)
    downs = tile_copies(down_send, down_recv, tile - 1, after, pres_after)

    for part in range(3):
        @pl.when(has_after)
        def _():
            ups[part].start()

        @pl.when(has_before)
        def _():
            downs[part].start()

    @pl.when(jnp.logical_not(has_before))
    def _():
        before[...] = jnp.zeros_like(before)
        pres_before[...] = jnp.zeros_like(pres_before)

    @pl.when(jnp.logical_not(has_after))
    def _():
        after[...] = jnp.zeros_like(after)
        pres_after[...] = jnp.zeros_like(pres_after)

    def arrived(part):
        @pl.when(has_before)
        def _():
            ups[part].wait_recv()

        @pl.when(has_after)
        def _():
            downs[part].wait_recv()

    pairs_copy.wait()
    invert_pairs(pairs, table_v, core, shard)

    tables = (table_a, table_b)

    def table_copy(unit):
        return pltpu.make_async_copy(table_v.at[8 * unit : 8 * unit + 8, :], tables[unit % 2], table_sem.at[unit % 2])

    table_copy(0).start()
    table_copy(1).start()
    outcome_copy.wait()
    turn_outcome(outcome, turned)

    own_copies[0].wait()
    speed_copy.wait()
    arrived(0)
    for k in range(LOCAL):
        moved = transported(own[0, k], before[0, k], after[0, k], jnp.full((8, 128), speed[k], f32))
        out[0, k] = moved
        dens[pl.ds(k, 8, stride=LOCAL), :] = moved

    def ring_copy(block, there, chunk, target, slot):
        make = lambda at: dens.at[at * 224 + chunk * 56 : at * 224 + chunk * 56 + 56, :]
        return pltpu.make_async_remote_copy(
            make(block), make(there), ring_send.at[slot], ring_recv.at[slot],
            device_id={"bins": target}, device_id_type=MESH,
        )

    forward, backward, relayed = (0, 1, 2, 3), (2, 3, 0, 1), (0, 2, 1, 3)
    to_nxt = [ring_copy(0, 2, c, nxt, c) for c in range(4)]
    to_prv = [ring_copy(0, 1, c, prv, 4 + c) for c in range(4)]
    relays = [ring_copy(2, 3, c, nxt, 8 + c) if c < 2 else ring_copy(1, 3, c, prv, 8 + c) for c in range(4)]
    sends = []
    for i in range(4):
        sends += [to_nxt[forward[i]], to_prv[backward[i]]]
    for copy in sends:
        copy.start()

    first_unit = core * UNITS
    other_unit = UNITS - first_unit

    def turn_copy(unit):
        piece = turns.at[pl.ds((first_unit + unit) * 4, 4)]
        return pltpu.make_async_remote_copy(
            piece, piece, turn_send.at[unit], turn_recv.at[unit],
            device_id={"tiles": tile + 1 - 2 * core}, device_id_type=MESH,
        )

    def arriving(unit):
        piece = turns.at[pl.ds((other_unit + unit) * 4, 4)]
        return pltpu.make_async_remote_copy(
            piece, piece, turn_send.at[unit], turn_recv.at[unit],
            device_id={"tiles": tile + 1 - 2 * core}, device_id_type=MESH,
        )

    def finish(unit, two):
        value = held[(unit % 2) * 4 + two].T[0:32, :]
        turns[(first_unit + unit) * 4 + two] = value
        place_two(value, rates, first_unit + unit, two)

    def sort_unit(unit):
        table_copy(unit).wait()
        for two in range(4):
            gather_two(tables[unit % 2], turned, held.at[(unit % 2) * 4 + two], two)
            if two > 0:
                finish(unit, two - 1)
            elif unit > 0:
                finish(unit - 1, 3)
        if unit > 0:
            turn_copy(unit - 1).start()
        if unit + 2 < UNITS:
            table_copy(unit + 2).start()

    def relay(c):
        (to_nxt if c < 2 else to_prv)[c].wait_recv()
        relays[c].start()

    def place_units(first, last):
        for unit in range(first, last):
            arriving(unit).wait_recv()

        def place_unit(unit, carry):
            for two in range(4):
                place_two(turns[(other_unit + unit) * 4 + two], rates, other_unit + unit, two)
            return carry

        lax.fori_loop(first, last, place_unit, 0)

    for unit in range(6):
        sort_unit(unit)
    relay(0)
    relay(2)
    sort_unit(6)
    finish(6, 3)
    place_units(0, 5)
    turn_copy(6).start()
    relay(1)
    relay(3)

    own_copies[1].wait()
    arrived(1)
    arrived(2)

    def momenta(k, carry):
        rate = jnp.full((8, 128), speed[k], f32)
        for d in range(1, 4):
            out[d, k] = transported(own[d, k], before[d, k], after[d, k], rate)
        return carry

    lax.fori_loop(0, LOCAL, momenta, 0)
    place_units(5, UNITS)

    for c in range(2):
        to_nxt[2 + c].wait_recv()
        to_prv[c].wait_recv()

    def split(c, groups):
        for m in (2 * c, 2 * c + 1):
            for group in groups:
                pieces, member = [], 0
                while member < 16:
                    b, w = bin_at(group, member)
                    size = 8 if w < 24 else 4
                    start = b * 224 + m * 28 + w
                    pieces.append(dens[start : start + size, :])
                    member += size
                value = jnp.concatenate(pieces, 0)
                top = value.astype(bf16)
                rest = (value - top.astype(f32)).astype(bf16)
                for at in (group, group + GROUPS):
                    if at < 10:
                        high[at * 16 : at * 16 + 16, m * 128 : m * 128 + 128] = top
                        low[at * 16 : at * 16 + 16, m * 128 : m * 128 + 128] = rest

    def multiply(c, groups, total):
        for group in groups:
            top = high[group * 16 : group * 16 + 64, c * 256 : c * 256 + 256]
            rest = low[group * 16 : group * 16 + 64, c * 256 : c * 256 + 256]
            weights = jnp.concatenate([top, top, rest, rest], 0)
            block = rates[group * 512 : group * 512 + 512, :]
            product = jnp.dot(jnp.concatenate([block, block], 1), weights, preferred_element_type=f32)
            for member in range(16):
                b, w = bin_at(group, member)
                start = b * 224 + w + c * 56
                line = jnp.concatenate([dens[start : start + 1, :], dens[start + 28 : start + 29, :]], 1)
                total += product[member * 32 : member * 32 + 32, :] * line
        return total

    for c in relayed:
        split(c, range(5))
        partial[c] = multiply(c, range(2), jnp.zeros((32, 256), f32))

    for c in relayed:
        relays[c].wait_recv()
        split(c, range(5, GROUPS))
        total = multiply(c, range(2, GROUPS), partial[c])
        for half in range(2):
            for k in range(4):
                source[pl.ds(k * 64 + 2 * c + half, 8, stride=8), :] = total[k * 8 : k * 8 + 8, half * 128 : half * 128 + 128]

    for copy in late_copies:
        copy.wait()
    row = lax.broadcasted_iota(i32, (8, 128), 0) & 3
    here_p = pres[...]
    above = jnp.where(row < 3, pltpu.roll(here_p, 7, 0), pltpu.roll(pres_after[...], 3, 0))
    below = jnp.where(row >= 1, pltpu.roll(here_p, 1, 0), pltpu.roll(pres_before[...], 5, 0))
    gradient = (above - below) / (2.0 * rho[...])
    gas = [vel[d] for d in range(3)]
    target = [gas[0] - gradient, gas[1], gas[2]]

    for k in range(LOCAL):
        half = 0.5 * source[k * 8 : k * 8 + 8, :]
        density = out[0, k] + half
        s = jnp.full((8, 128), stop[k], f32)
        share = 1.0 / (1.0 + s)
        pull = s * density
        out[0, k] = density
        for d in range(3):
            grown = out[d + 1, k] + half * gas[d]
            out[d + 1, k] = (grown + pull * target[d]) * share

    for copy in (*sends, *relays, *[turn_copy(unit) for unit in range(UNITS)]):
        copy.wait_send()
    for part in range(3):
        @pl.when(has_after)
        def _():
            ups[part].wait_send()

        @pl.when(has_before)
        def _():
            downs[part].wait_send()


def folded(value):
    lead = value.shape[:-2]
    value = value.reshape(*lead, 4, 2, 128)
    return jnp.swapaxes(value, -3, -2).reshape(*lead, 8, 128)


def unfolded(value):
    lead = value.shape[:-2]
    value = value.reshape(*lead, 2, 4, 128)
    return jnp.swapaxes(value, -3, -2).reshape(*lead, 4, 256)


def local(dust_state, drift_speed, stop_ratio, gas_rho, gas_vel, pressure, pair_list, outcome):
    halo = pltpu.VMEM((4, LOCAL, 8, 128), f32)
    cell = pltpu.VMEM((8, 128), f32)
    dma = pltpu.SemaphoreType.DMA
    result = pl.pallas_call(
        step_kernel,
        out_shape=pltpu.VMEM((4, LOCAL, 8, 128), f32),
        in_specs=[pl.BlockSpec(memory_space=pl.ANY)] * 8,
        out_specs=pl.BlockSpec(memory_space=pltpu.VMEM),
        scratch_shapes=[
            halo, halo, halo, cell, cell,
            pltpu.VMEM((4 * 224, 128), f32),
            pltpu.VMEM((160, 1024), bf16),
            pltpu.VMEM((160, 1024), bf16),
            pltpu.VMEM((4, 32, 256), f32),
            pltpu.VMEM((256, 128), f32),
            pltpu.SMEM((LOCAL,), f32),
            pltpu.SMEM((LOCAL,), f32),
            cell,
            pltpu.VMEM((3, 8, 128), f32),
            cell,
            pltpu.VMEM((2, PAIRS), i32),
            pltpu.VMEM((LOCAL, PAIRS), f32),
            pltpu.VMEM((PAIRS, 128), f32),
            pltpu.VMEM((8, 128, 128), f32),
            pltpu.VMEM((2 * UNITS * 4, 32, 128), f32),
            pltpu.VMEM((HALF, 128), i32),
            pltpu.SMEM((8, 128), i32),
            pltpu.SMEM((8, 128), i32),
            pltpu.VMEM((BINS * 32, 128), bf16),
            dma((2,)), dma((7,)), dma((2,)),
            dma((3,)), dma((3,)), dma((3,)), dma((3,)),
            dma((12,)), dma((12,)), dma((UNITS,)), dma((UNITS,)),
        ],
        compiler_params=pltpu.CompilerParams(collective_id=0, has_side_effects=True),
        name="dust_step",
    )(
        folded(dust_state), drift_speed, stop_ratio, folded(gas_rho), folded(gas_vel), folded(pressure),
        pair_list.T, outcome.T,
    )
    return unfolded(result)


def solution(mesh):
    return jax.shard_map(
        local,
        mesh=mesh,
        in_specs=(
            P(None, "bins", "tiles", None),
            P("bins"),
            P("bins"),
            P("tiles", None),
            P(None, "tiles", None),
            P("tiles", None),
            P(),
            P(None, "bins"),
        ),
        out_specs=P(None, "bins", "tiles", None),
        check_vma=False,
    )
```

```python
import functools

import jax
import jax.numpy as jnp
from jax import lax
from jax.experimental import pallas as pl
from jax.experimental.pallas import tpu as pltpu
from jax.sharding import PartitionSpec as P

MESH = pl.DeviceIdType.MESH
BINS = 112
LOCAL = 28
PAIRS = 6328
HALF = BINS // 2
UNITS = 7
GROUPS = 7
f32, bf16, i32 = jnp.float32, jnp.bfloat16, jnp.int32


def bin_at(group, member):
    tile, low = 2 * group + member // 8, member % 8
    if tile < 9:
        return tile // 3, (tile % 3) * 8 + low
    if tile == 9:
        return low // 4, 24 + low % 4
    if tile < 13:
        return 3, (tile - 10) * 8 + low
    return 2 + low // 4, 24 + low % 4


def group_member(index, shard):
    owner = (index >= 28).astype(i32) + (index >= 56).astype(i32) + (index >= 84).astype(i32)
    own = index - 28 * owner
    ahead = (owner - shard) & 3
    block = jnp.where(ahead == 2, 3, jnp.where(ahead == 3, 2, ahead))
    full = jnp.where(block == 3, 10, 3 * block) + (own >> 3)
    left = jnp.where(block < 2, 9, 13)
    is_full = own < 24
    tile = jnp.where(is_full, full, left)
    low = jnp.where(is_full, own & 7, ((block & 1) << 2) + own - 24)
    return tile >> 1, ((tile & 1) << 3) + low


def slots_of(pairs, shard):
    group_i, member_i = group_member(pairs[0:1, :], shard)
    group_j, member_j = group_member(pairs[1:2, :], shard)
    ahead = group_j - group_i
    ahead = jnp.where(ahead < 0, ahead + GROUPS, ahead)
    keep = (ahead <= 3) & ((ahead > 0) | (member_i <= member_j))
    ahead = jnp.where((ahead == 0) & ~keep, GROUPS, ahead)
    row = jnp.where(keep, group_i * 16 + member_i, group_j * 16 + member_j)
    slot = jnp.where(keep, ahead * 16 + member_j, (GROUPS - ahead) * 16 + member_i)
    return row, slot


def invert_pairs(pairs_ref, table_ref, core, shard):
    total = jnp.zeros((HALF, 128), f32)
    for start in range(0, PAIRS, 256):
        width = min(256, PAIRS - start)
        row, slot = slots_of(pairs_ref[:, start : start + width], shard)
        rows = lax.broadcasted_iota(i32, (HALF, width), 0)
        lanes = lax.broadcasted_iota(i32, (128, width), 0)
        number = start + 1 + lax.broadcasted_iota(i32, (1, width), 1)
        high = (number >> 6).astype(f32)
        low = (number & 63).astype(f32)
        value = jnp.where(lanes < 64, high, low)
        first = jnp.where(rows == row - HALF * core, 1.0, 0.0).astype(bf16)
        second = jnp.where((lanes & 63) == slot, value, 0.0).astype(bf16)
        total += lax.dot_general(first, second, (((1,), (1,)), ((), ())), preferred_element_type=f32)
    number = total * 64.0 + pltpu.roll(total, 64, 1)
    table_ref[...] = jnp.clip(number.astype(i32) - 1, 0, PAIRS - 1)


def turn_outcome(outcome_ref, turned_ref):
    for start in range(0, PAIRS, 128):
        width = min(128, PAIRS - start)
        turned_ref[start : start + width, 0:LOCAL] = outcome_ref[:, start : start + width].T


def gather_two(table, turned, held, two):
    for half in range(2):
        member = 2 * two + half
        for slot in range(member, 64):
            at = half * 64 + slot
            index = table[member, slot]
            held[at : at + 1, :] = turned[pl.ds(index, 1), :]


def place_two(value, rates, unit, two):
    lane = lax.broadcasted_iota(i32, (32, 128), 1)
    left = lane < 64
    member = lax.rem(unit, 2) * 8 + 2 * two
    value = jnp.where((lane & 63) < jnp.where(left, member, member + 1), 0.0, value)
    high = value.astype(bf16).astype(f32)
    low = pltpu.roll(value - high, 64, 1)
    start = pl.multiple_of(unit * 256 + two * 64, 64)
    rates[pl.ds(start, 32), :] = jnp.where(left, high, low).astype(bf16)
    rates[pl.ds(start + 32, 32), :] = jnp.where(left, low, high).astype(bf16)


def transported(own, before, after, speed):
    forward = jnp.maximum(speed, 0.0)
    backward = jnp.maximum(-speed, 0.0)

    def weights(a):
        square = a * a
        return (2.0 * a - 3.0 * square, 2.75 * square - 0.5 * a, -square, 0.125 * square)

    a = forward + backward
    row = lax.broadcasted_iota(i32, (8, 128), 0) & 3
    result = (1.0 - 1.5 * a + 1.125 * (a * a)) * own
    up, down = weights(forward), weights(backward)
    before_swap, after_swap = pltpu.roll(before, 4, 0), pltpu.roll(after, 4, 0)
    for m in (1, 2, 3):
        result += up[m - 1] * pltpu.roll(jnp.where(row < 4 - m, own, before_swap), m, 0)
        result += down[m - 1] * pltpu.roll(jnp.where(row >= m, own, after_swap), 8 - m, 0)
    return result + up[3] * before + down[3] * after


def step_kernel(
    dust_in, speed_in, stop_in, rho_in, vel_in, pres_in, pairs_in, outcome_in, out,
    own, before, after, pres_before, pres_after, dens, high, low, partial, source,
    speed, stop, rho, vel, pres, pairs, outcome,
    turned, held, turns, table_v, table_a, table_b, rates,
    own_sem, in_sem, table_sem, up_send, up_recv, down_send, down_recv, ring_send, ring_recv, turn_send, turn_recv,
):
    tile, shard = lax.axis_index("tiles"), lax.axis_index("bins")
    tiles, shards = lax.axis_size("tiles"), lax.axis_size("bins")
    has_before, has_after = tile > 0, tile < tiles - 1
    core = lax.rem(tile, 2)
    nxt, prv = lax.rem(shard + 1, shards), lax.rem(shard + shards - 1, shards)

    barrier = pltpu.get_barrier_semaphore()
    pl.semaphore_signal(barrier, inc=1, device_id={"bins": nxt}, device_id_type=MESH)
    pl.semaphore_signal(barrier, inc=1, device_id={"bins": prv}, device_id_type=MESH)

    @pl.when(has_before)
    def _():
        pl.semaphore_signal(barrier, inc=1, device_id={"tiles": tile - 1}, device_id_type=MESH)

    @pl.when(has_after)
    def _():
        pl.semaphore_signal(barrier, inc=1, device_id={"tiles": tile + 1}, device_id_type=MESH)

    own_copies = [
        pltpu.make_async_copy(dust_in.at[0:1], own.at[0:1], own_sem.at[0]),
        pltpu.make_async_copy(dust_in.at[1:4], own.at[1:4], own_sem.at[1]),
    ]
    moves = ((pairs_in, pairs), (speed_in, speed), (outcome_in, outcome), (stop_in, stop), (rho_in, rho), (vel_in, vel), (pres_in, pres))
    pairs_copy, speed_copy, outcome_copy, *late_copies = [
        pltpu.make_async_copy(source_ref, target_ref, in_sem.at[i]) for i, (source_ref, target_ref) in enumerate(moves)
    ]
    pairs_copy.start()
    own_copies[0].start()
    speed_copy.start()
    outcome_copy.start()
    own_copies[1].start()
    for copy in late_copies:
        copy.start()

    pl.semaphore_wait(barrier, 2 + has_before.astype(i32) + has_after.astype(i32))

    def tile_copies(send, recv, target, there, pres_there):
        make = functools.partial(pltpu.make_async_remote_copy, device_id={"tiles": target}, device_id_type=MESH)
        return [
            make(dust_in.at[0:1], there.at[0:1], send.at[0], recv.at[0]),
            make(pres_in, pres_there, send.at[1], recv.at[1]),
            make(dust_in.at[1:4], there.at[1:4], send.at[2], recv.at[2]),
        ]

    ups = tile_copies(up_send, up_recv, tile + 1, before, pres_before)
    downs = tile_copies(down_send, down_recv, tile - 1, after, pres_after)

    for part in range(3):
        @pl.when(has_after)
        def _():
            ups[part].start()

        @pl.when(has_before)
        def _():
            downs[part].start()

    @pl.when(jnp.logical_not(has_before))
    def _():
        before[...] = jnp.zeros_like(before)
        pres_before[...] = jnp.zeros_like(pres_before)

    @pl.when(jnp.logical_not(has_after))
    def _():
        after[...] = jnp.zeros_like(after)
        pres_after[...] = jnp.zeros_like(pres_after)

    def arrived(part):
        @pl.when(has_before)
        def _():
            ups[part].wait_recv()

        @pl.when(has_after)
        def _():
            downs[part].wait_recv()

    pairs_copy.wait()
    invert_pairs(pairs, table_v, core, shard)

    tables = (table_a, table_b)

    def table_copy(unit):
        return pltpu.make_async_copy(table_v.at[8 * unit : 8 * unit + 8, :], tables[unit % 2], table_sem.at[unit % 2])

    table_copy(0).start()
    table_copy(1).start()
    outcome_copy.wait()
    turn_outcome(outcome, turned)

    own_copies[0].wait()
    speed_copy.wait()
    arrived(0)
    for k in range(LOCAL):
        moved = transported(own[0, k], before[0, k], after[0, k], jnp.full((8, 128), speed[k], f32))
        out[0, k] = moved
        dens[pl.ds(k, 8, stride=LOCAL), :] = moved

    def ring_copy(block, there, chunk, target, slot):
        make = lambda at: dens.at[at * 224 + chunk * 56 : at * 224 + chunk * 56 + 56, :]
        return pltpu.make_async_remote_copy(
            make(block), make(there), ring_send.at[slot], ring_recv.at[slot],
            device_id={"bins": target}, device_id_type=MESH,
        )

    forward, backward, relayed = (0, 1, 2, 3), (2, 3, 0, 1), (0, 2, 1, 3)
    to_nxt = [ring_copy(0, 2, c, nxt, c) for c in range(4)]
    to_prv = [ring_copy(0, 1, c, prv, 4 + c) for c in range(4)]
    relays = [ring_copy(2, 3, c, nxt, 8 + c) if c < 2 else ring_copy(1, 3, c, prv, 8 + c) for c in range(4)]
    sends = []
    for i in range(4):
        sends += [to_nxt[forward[i]], to_prv[backward[i]]]
    for copy in sends[0:4]:
        copy.start()

    first_unit = core * UNITS
    other_unit = UNITS - first_unit

    def turn_copy(unit):
        piece = turns.at[pl.ds((first_unit + unit) * 4, 4)]
        return pltpu.make_async_remote_copy(
            piece, piece, turn_send.at[unit], turn_recv.at[unit],
            device_id={"tiles": tile + 1 - 2 * core}, device_id_type=MESH,
        )

    def arriving(unit):
        piece = turns.at[pl.ds((other_unit + unit) * 4, 4)]
        return pltpu.make_async_remote_copy(
            piece, piece, turn_send.at[unit], turn_recv.at[unit],
            device_id={"tiles": tile + 1 - 2 * core}, device_id_type=MESH,
        )

    def finish(unit, two):
        value = held[(unit % 2) * 4 + two].T[0:32, :]
        turns[(first_unit + unit) * 4 + two] = value
        place_two(value, rates, first_unit + unit, two)

    def sort_unit(unit):
        table_copy(unit).wait()
        for two in range(4):
            gather_two(tables[unit % 2], turned, held.at[(unit % 2) * 4 + two], two)
            if two > 0:
                finish(unit, two - 1)
            elif unit > 0:
                finish(unit - 1, 3)
        if unit > 0:
            turn_copy(unit - 1).start()
        if unit + 2 < UNITS:
            table_copy(unit + 2).start()

    def relay(c):
        (to_nxt if c < 2 else to_prv)[c].wait_recv()
        relays[c].start()

    def place_units(first, last):
        for unit in range(first, last):
            arriving(unit).wait_recv()

        def place_unit(unit, carry):
            for two in range(4):
                place_two(turns[(other_unit + unit) * 4 + two], rates, other_unit + unit, two)
            return carry

        lax.fori_loop(first, last, place_unit, 0)

    for unit in range(6):
        sort_unit(unit)
        if unit == 1:
            sends[4].start()
            sends[5].start()
    relay(0)
    relay(2)
    sends[6].start()
    sends[7].start()
    sort_unit(6)
    finish(6, 3)
    place_units(0, 5)
    turn_copy(6).start()
    relay(1)
    relay(3)

    own_copies[1].wait()
    arrived(1)
    arrived(2)

    def momenta(k, carry):
        rate = jnp.full((8, 128), speed[k], f32)
        for d in range(1, 4):
            out[d, k] = transported(own[d, k], before[d, k], after[d, k], rate)
        return carry

    lax.fori_loop(0, LOCAL, momenta, 0)
    place_units(5, UNITS)

    for c in range(2):
        to_nxt[2 + c].wait_recv()
        to_prv[c].wait_recv()

    def split(c, groups):
        for m in (2 * c, 2 * c + 1):
            for group in groups:
                pieces, member = [], 0
                while member < 16:
                    b, w = bin_at(group, member)
                    size = 8 if w < 24 else 4
                    start = b * 224 + m * 28 + w
                    pieces.append(dens[start : start + size, :])
                    member += size
                value = jnp.concatenate(pieces, 0)
                top = value.astype(bf16)
                rest = (value - top.astype(f32)).astype(bf16)
                for at in (group, group + GROUPS):
                    if at < 10:
                        high[at * 16 : at * 16 + 16, m * 128 : m * 128 + 128] = top
                        low[at * 16 : at * 16 + 16, m * 128 : m * 128 + 128] = rest

    def multiply(c, groups, total):
        for group in groups:
            top = high[group * 16 : group * 16 + 64, c * 256 : c * 256 + 256]
            rest = low[group * 16 : group * 16 + 64, c * 256 : c * 256 + 256]
            weights = jnp.concatenate([top, top, rest, rest], 0)
            block = rates[group * 512 : group * 512 + 512, :]
            product = jnp.dot(jnp.concatenate([block, block], 1), weights, preferred_element_type=f32)
            for member in range(16):
                b, w = bin_at(group, member)
                start = b * 224 + w + c * 56
                line = jnp.concatenate([dens[start : start + 1, :], dens[start + 28 : start + 29, :]], 1)
                total += product[member * 32 : member * 32 + 32, :] * line
        return total

    for c in relayed:
        split(c, range(5))
        partial[c] = multiply(c, range(2), jnp.zeros((32, 256), f32))

    for c in relayed:
        relays[c].wait_recv()
        split(c, range(5, GROUPS))
        total = multiply(c, range(2, GROUPS), partial[c])
        for half in range(2):
            for k in range(4):
                source[pl.ds(k * 64 + 2 * c + half, 8, stride=8), :] = total[k * 8 : k * 8 + 8, half * 128 : half * 128 + 128]

    for copy in late_copies:
        copy.wait()
    row = lax.broadcasted_iota(i32, (8, 128), 0) & 3
    here_p = pres[...]
    above = jnp.where(row < 3, pltpu.roll(here_p, 7, 0), pltpu.roll(pres_after[...], 3, 0))
    below = jnp.where(row >= 1, pltpu.roll(here_p, 1, 0), pltpu.roll(pres_before[...], 5, 0))
    gradient = (above - below) / (2.0 * rho[...])
    gas = [vel[d] for d in range(3)]
    target = [gas[0] - gradient, gas[1], gas[2]]

    for k in range(LOCAL):
        half = 0.5 * source[k * 8 : k * 8 + 8, :]
        density = out[0, k] + half
        s = jnp.full((8, 128), stop[k], f32)
        share = 1.0 / (1.0 + s)
        pull = s * density
        out[0, k] = density
        for d in range(3):
            grown = out[d + 1, k] + half * gas[d]
            out[d + 1, k] = (grown + pull * target[d]) * share

    for copy in (*sends, *relays, *[turn_copy(unit) for unit in range(UNITS)]):
        copy.wait_send()
    for part in range(3):
        @pl.when(has_after)
        def _():
            ups[part].wait_send()

        @pl.when(has_before)
        def _():
            downs[part].wait_send()


def folded(value):
    lead = value.shape[:-2]
    value = value.reshape(*lead, 4, 2, 128)
    return jnp.swapaxes(value, -3, -2).reshape(*lead, 8, 128)


def unfolded(value):
    lead = value.shape[:-2]
    value = value.reshape(*lead, 2, 4, 128)
    return jnp.swapaxes(value, -3, -2).reshape(*lead, 4, 256)


def local(dust_state, drift_speed, stop_ratio, gas_rho, gas_vel, pressure, pair_list, outcome):
    halo = pltpu.VMEM((4, LOCAL, 8, 128), f32)
    cell = pltpu.VMEM((8, 128), f32)
    dma = pltpu.SemaphoreType.DMA
    result = pl.pallas_call(
        step_kernel,
        out_shape=pltpu.VMEM((4, LOCAL, 8, 128), f32),
        in_specs=[pl.BlockSpec(memory_space=pl.ANY)] * 8,
        out_specs=pl.BlockSpec(memory_space=pltpu.VMEM),
        scratch_shapes=[
            halo, halo, halo, cell, cell,
            pltpu.VMEM((4 * 224, 128), f32),
            pltpu.VMEM((160, 1024), bf16),
            pltpu.VMEM((160, 1024), bf16),
            pltpu.VMEM((4, 32, 256), f32),
            pltpu.VMEM((256, 128), f32),
            pltpu.SMEM((LOCAL,), f32),
            pltpu.SMEM((LOCAL,), f32),
            cell,
            pltpu.VMEM((3, 8, 128), f32),
            cell,
            pltpu.VMEM((2, PAIRS), i32),
            pltpu.VMEM((LOCAL, PAIRS), f32),
            pltpu.VMEM((PAIRS, 128), f32),
            pltpu.VMEM((8, 128, 128), f32),
            pltpu.VMEM((2 * UNITS * 4, 32, 128), f32),
            pltpu.VMEM((HALF, 128), i32),
            pltpu.SMEM((8, 128), i32),
            pltpu.SMEM((8, 128), i32),
            pltpu.VMEM((BINS * 32, 128), bf16),
            dma((2,)), dma((7,)), dma((2,)),
            dma((3,)), dma((3,)), dma((3,)), dma((3,)),
            dma((12,)), dma((12,)), dma((UNITS,)), dma((UNITS,)),
        ],
        compiler_params=pltpu.CompilerParams(collective_id=0, has_side_effects=True),
        name="dust_step",
    )(
        folded(dust_state), drift_speed, stop_ratio, folded(gas_rho), folded(gas_vel), folded(pressure),
        pair_list.T, outcome.T,
    )
    return unfolded(result)


def solution(mesh):
    return jax.shard_map(
        local,
        mesh=mesh,
        in_specs=(
            P(None, "bins", "tiles", None),
            P("bins"),
            P("bins"),
            P("tiles", None),
            P(None, "tiles", None),
            P("tiles", None),
            P(),
            P(None, "bins"),
        ),
        out_specs=P(None, "bins", "tiles", None),
        check_vma=False,
    )
```
